256 devices in a mesh: sub: 64 (over z, x, y_hi), mode: 4 (over y_lo, core).
Axes of the slice: x: 4, y: 4 (y_hi: 2, y_lo: 2; y = y_hi * 2 + y_lo), z: 8, core: 2. Of those that a mesh axis runs over, the one named last changes fastest.
Arguments:
- right_side: float32 [2048, 32768], P('mode', 'sub'), may hold values from -6 to 6
- start_field: float32 [2048, 32768], P('mode', 'sub'), may hold values from -6 to 6
- coefficient: float32 [4, 32768], P(None, 'sub'), may hold values from 0.1 to 1
- gblocks: bfloat16 [4, 16, 4, 128, 128], P(None, 'mode'), may hold values from -0.125 to 0.125
- pattern: int32 [4, 16, 4], replicated, may hold values from 0 to 15, as said below
- sub_inverse: bfloat16 [32768, 512], P('sub'), may hold values from -0.125 to 0.125
- coarse_index: int32 [1024], P('sub'), may hold values from 0 to 511, as said below
- coarse_inv: float32 [1024, 16], P('sub'), may hold values from -1.5 to 1.5
- coupling: float32 [1024, 16], P('sub'), may hold values from -1 to 1
Outputs:
- field: float32 [2048, 32768], P('mode', 'sub')
- residual: float32 [2048, 32768], P('mode', 'sub')
The draws below stay inside these ranges and needn't reach their ends.
Inputs may be any that keep to these rules, and one draw needn't show every extreme that they name: pattern[k, c, 0] = c, and the 4 entries of pattern[k, c] are distinct. `coarse_index`: the 16 entries of one subdomain are distinct.
All inputs are finite; a program needn't handle non-finite values.
Results may differ from the reference program's by a relative error of at most 0.0036.
Values may be sent and summed in bfloat16 or wider, within the bound.
No kernel may reach another device: no remote copies, remote signals or barrier semaphores. Data moves between devices by JAX's collectives and lax.ppermute only.
A program may use at most 64 MiB of HBM per device.

```python
import math
import jax
import jax.numpy as jnp
from jax import lax

MODES = 2048
BLOCK = 128
NNZ = 4
KL = 4
NODES_DEV = 512
COARSE_DEV = 16
ITERS = 2
NBLK = 16
NODES = 32768
NCOARSE = 1024


def draw_pattern(key, part):
    nblocks = MODES // BLOCK
    key_list = jax.random.split(jax.random.fold_in(key, 5), KL * nblocks)
    shuffled = jax.vmap(lambda subkey: jax.random.permutation(subkey, nblocks - 1))(key_list)
    column_block = jnp.arange(KL * nblocks) % nblocks
    others = shuffled[:, :NNZ - 1]
    others = others + (others >= column_block[:, None]).astype(others.dtype)
    joined = jnp.concatenate([column_block[:, None].astype(others.dtype), others], axis=1)
    return joined.reshape(KL, nblocks, NNZ).astype(jnp.int32)


def draw_coarse_index(key, part):
    subdomains = NCOARSE // COARSE_DEV
    key_list = jax.random.split(jax.random.fold_in(key, 7), subdomains)
    shuffled = jax.vmap(lambda subkey: jax.random.permutation(subkey, NODES_DEV - 2))(key_list)
    chosen = shuffled[:, :COARSE_DEV] + 1
    chosen = chosen.at[0, 0].set(0).at[0, 1].set(NODES_DEV - 1)
    return chosen.reshape(-1).astype(jnp.int32)


def draw_coupling(key, part):
    first_key, second_key = jax.random.split(jax.random.fold_in(key, 11))
    diagonal = jax.random.uniform(first_key, (NCOARSE,), jnp.float32, 0.8, 0.97)
    offdiag = jax.random.normal(second_key, (NCOARSE, COARSE_DEV), jnp.float32) * (0.06 / COARSE_DEV ** 0.5)
    on_diagonal = (jnp.arange(NCOARSE) % COARSE_DEV)[:, None] == jnp.arange(COARSE_DEV)[None, :]
    return jnp.clip(jnp.where(on_diagonal, diagonal[:, None], offdiag), -1.0, 1.0).astype(jnp.float32)


def level_of(own_key, shape, pieces, low, high):
    def one(dim, shards_of):
        steps = jax.random.uniform(jax.random.fold_in(jax.random.fold_in(own_key, 6), dim), (shards_of,), jnp.float32, low / len(pieces), high / len(pieces))
        return jnp.repeat(jnp.exp(steps), shape[dim] // shards_of).reshape((-1,) + (1,) * (len(shape) - dim - 1))

    gain = one(*pieces[0])
    for cut in pieces[1:]:
        gain = gain * one(*cut)
    return gain


def centred(key, extent, width, bound, pieces=(), kind=jnp.bfloat16):
    array = width * jax.random.normal(key, extent, jnp.float32)
    if pieces:
        array = array * level_of(key, extent, pieces, -0.22, 0.18)
    return jnp.clip(array, -bound, bound).astype(kind)


def setup_inputs(seed: int = 0) -> dict:
    key_of = jax.random.split(jax.random.key(seed), 10)
    return {
        "right_side": centred(key_of[0], (MODES, NODES), 1.0, 6.0, ((0, 4), (1, 64)), jnp.float32),
        "start_field": centred(key_of[1], (MODES, NODES), 1.0, 6.0, ((0, 4), (1, 64)), jnp.float32),
        "coefficient": jnp.clip(jnp.exp(math.log(1.0) - 2.3025851 * jax.random.uniform(key_of[2], (KL, NODES), jnp.float32) ** level_of(key_of[2], (KL, NODES), ((1, 64),), -0.2, 0.2)), 0.1, 1.0),
        "gblocks": centred(key_of[3], (KL, NBLK, NNZ, BLOCK, BLOCK), (4 * NNZ * BLOCK) ** -0.5, 0.125, ((1, 4),)),
        "pattern": draw_pattern(jax.random.fold_in(key_of[9], 71), 0),
        "sub_inverse": centred(key_of[5], (NODES, NODES_DEV), (4 * NODES_DEV) ** -0.5, 0.125, ((0, 64),)),
        "coarse_index": draw_coarse_index(jax.random.fold_in(key_of[9], 71), 0),
        "coarse_inv": centred(key_of[7], (NCOARSE, COARSE_DEV), COARSE_DEV ** -0.5, 1.5, ((0, 64),), jnp.float32),
        "coupling": draw_coupling(jax.random.fold_in(key_of[9], 71), 0),
    }


def second_difference(values):
    padded = jnp.pad(values, ((0, 0), (1, 1)))
    return 2.0 * values - padded[:, :-2] - padded[:, 2:]


def reference(right_side, start_field, coefficient, gblocks, pattern, sub_inverse, coarse_index, coarse_inv, coupling):
    highest = lax.Precision.HIGHEST
    modes, nodes = right_side.shape
    nblocks = modes // BLOCK
    subdomains = nodes // NODES_DEV
    node_range = jnp.arange(NODES_DEV).astype(jnp.int32)
    onehot = (coarse_index.reshape(subdomains, COARSE_DEV)[:, :, None] == node_range[None, None, :]).astype(jnp.float32)
    inv_blocks = sub_inverse.reshape(subdomains, NODES_DEV, NODES_DEV).astype(jnp.float32)
    cinv_blocks = coarse_inv.reshape(subdomains, COARSE_DEV, COARSE_DEV)
    coup_blocks = coupling.reshape(subdomains, COARSE_DEV, COARSE_DEV)
    field = start_field
    residual = right_side
    for turn_index in range(ITERS):
        diffs = second_difference(field).astype(jnp.bfloat16)
        diff_blocks = diffs.reshape(nblocks, BLOCK, nodes)
        operated = jnp.zeros((modes, nodes), jnp.float32)
        for term in range(KL):
            def column(column_block):
                rows = diff_blocks[pattern[term, column_block]].astype(jnp.float32)
                stored = gblocks[term, column_block].astype(jnp.float32)
                return jnp.einsum('tbn,tbc->cn', rows, stored)
            product = lax.map(column, jnp.arange(nblocks).astype(jnp.int32)).reshape(modes, nodes)
            operated = operated + coefficient[term][None, :] * product
        residual = right_side - operated
        rounded = residual.astype(jnp.bfloat16).astype(jnp.float32).reshape(modes, subdomains, NODES_DEV)
        local = jnp.einsum('msp,spq->msq', rounded, inv_blocks, precision=highest).reshape(modes, nodes)
        split_res = residual.reshape(modes, subdomains, NODES_DEV)
        restricted = jnp.einsum('msn,scn->msc', split_res, onehot, precision=highest)
        feed = jnp.einsum('msc,scd->msd', restricted, cinv_blocks, precision=highest)

        def advance(carry, inputs):
            coup, push = inputs
            moved = jnp.dot(carry, coup, precision=highest) + push
            return moved, moved

        last_error, errors = lax.scan(advance, jnp.zeros((modes, COARSE_DEV), jnp.float32), (coup_blocks, jnp.transpose(feed, (1, 0, 2))))
        error = jnp.transpose(errors, (1, 0, 2))
        prolonged = jnp.einsum('msc,scn->msn', error, onehot, precision=highest).reshape(modes, nodes)
        field = field + local + prolonged
    return field, residual
```

```python
import functools

import jax
import jax.numpy as jnp
from jax import lax
from jax.experimental import pallas as pl
from jax.experimental.pallas import tpu as pltpu
from jax.sharding import Mesh
from jax.sharding import PartitionSpec as P

SUB = ("z", "x", "yh")
PLANE = ("x", "yh")
MODE = ("yl", "core")
EDGE = 32
LANES = 128
F32 = jnp.float32
BF16 = jnp.bfloat16
VMEM = pl.BlockSpec(memory_space=pltpu.VMEM)
SMEM = pl.BlockSpec(memory_space=pltpu.SMEM)


def params(mib):
    return pltpu.CompilerParams(vmem_limit_bytes=mib * 2**20)


def shape(dims, dtype=F32):
    return jax.ShapeDtypeStruct(dims, dtype)


def start_kernel(field_ref, middle_ref, top_ref, low_ref, last_ref, first_ref):
    field = jnp.transpose(field_ref[...])
    nodes = field.shape[0]
    diffs = 2.0 * field - pltpu.roll(field, 1, 0) - pltpu.roll(field, nodes - 1, 0)
    middle_ref[...] = diffs[EDGE : nodes - EDGE].astype(BF16)
    top_ref[...] = field[: EDGE + 8]
    low_ref[...] = field[nodes - EDGE - 8 :]
    last_ref[...] = jnp.broadcast_to(field[nodes - 1 :], last_ref.shape)
    first_ref[...] = jnp.broadcast_to(field[:1], first_ref.shape)


def start(field):
    modes, nodes = field.shape
    column = lambda rows: pl.BlockSpec((rows, LANES), lambda j: (0, j))
    return pl.pallas_call(
        start_kernel,
        grid=(modes // LANES,),
        in_specs=[pl.BlockSpec((LANES, nodes), lambda j: (j, 0))],
        out_specs=[column(nodes - 2 * EDGE), column(EDGE + 8), column(EDGE + 8), column(8), column(8)],
        out_shape=[
            shape((nodes - 2 * EDGE, modes), BF16),
            shape((EDGE + 8, modes)),
            shape((EDGE + 8, modes)),
            shape((8, modes)),
            shape((8, modes)),
        ],
        name="start",
    )(field)


def affected(index_ref, nodes):
    found = []
    for c in range(index_ref.shape[0]):
        for off in (-1, 0, 1):
            found.append(jnp.clip(index_ref[c] + off, 0, nodes - 1))
    return found + [0, nodes - 1]


def around(index_ref, nodes):
    found = []
    for c in range(index_ref.shape[0]):
        for off in (-2, -1, 0, 1, 2):
            found.append(jnp.clip(index_ref[c] + off, 0, nodes - 1))
    return found + [0, 1, nodes - 2, nodes - 1]


def padded(count):
    return -(-count // 16) * 16


def at(row):
    return slice(row, row + 1) if isinstance(row, int) else pl.ds(row, 1)


def prepare_kernel(index_ref, right_ref, inverse_ref, field_ref, coef_ref, right_t_ref, inverse_t_ref, field_t_ref, coef_t_ref, right_rows_ref, coef_rows_ref):
    right_t_ref[...] = jnp.transpose(right_ref[...])
    inverse_t_ref[...] = jnp.transpose(inverse_ref[...].astype(F32)).astype(BF16)
    field_t_ref[...] = jnp.transpose(field_ref[...])
    terms, nodes = coef_ref.shape
    found = affected(index_ref, nodes)
    right_rows_ref[...] = jnp.zeros_like(right_rows_ref)
    for j, n in enumerate(found):
        right_rows_ref[j : j + 1] = right_t_ref[at(n), :]

    @pl.when(pl.program_id(0) == 0)
    def _():
        wide = jnp.concatenate([coef_ref[...], jnp.zeros((LANES - terms, nodes), F32)], axis=0)
        coef_t_ref[...] = jnp.transpose(wide)
        coef_rows_ref[...] = jnp.zeros_like(coef_rows_ref)
        for j, n in enumerate(found):
            coef_rows_ref[j : j + 1] = coef_t_ref[at(n), :]


def prepare(index, right_side, sub_inverse, field, coefficient):
    modes, nodes = right_side.shape
    count = padded(3 * index.shape[0] + 2)
    rows = lambda width: pl.BlockSpec((LANES, width), lambda j: (j, 0))
    column = lambda height: pl.BlockSpec((height, LANES), lambda j: (0, j))
    fixed = lambda height: pl.BlockSpec((height, LANES), lambda j: (0, 0))
    return pl.pallas_call(
        prepare_kernel,
        grid=(modes // LANES,),
        in_specs=[
            SMEM,
            rows(nodes),
            rows(nodes),
            rows(nodes),
            pl.BlockSpec(coefficient.shape, lambda j: (0, 0)),
        ],
        out_specs=[column(nodes)] * 3 + [fixed(nodes), column(count), fixed(count)],
        out_shape=[
            shape((nodes, modes)),
            shape((nodes, nodes), BF16),
            shape((nodes, modes)),
            shape((nodes, LANES)),
            shape((count, modes)),
            shape((count, LANES)),
        ],
        name="prepare",
    )(index, right_side, sub_inverse, field, coefficient)


def edge_kernel(top_ref, low_ref, left_ref, right_ref, edge_ref):
    top = top_ref[...]
    before = jnp.concatenate([left_ref[:1], top[: EDGE - 1]], axis=0)
    edge_ref[:EDGE] = (2.0 * top[:EDGE] - before - top[1 : EDGE + 1]).astype(BF16)
    low = low_ref[...]
    after = jnp.concatenate([low[9:], right_ref[:1]], axis=0)
    edge_ref[EDGE:] = (2.0 * low[8:] - low[7:-1] - after).astype(BF16)


def edges(top, low, left, right):
    return pl.pallas_call(
        edge_kernel,
        in_specs=[VMEM] * 4,
        out_specs=VMEM,
        out_shape=shape((2 * EDGE, top.shape[1]), BF16),
        compiler_params=params(16),
        name="edges",
    )(top, low, left, right)


HBM = pl.BlockSpec(memory_space=pltpu.HBM)
ANY = pl.BlockSpec(memory_space=pl.ANY)


def copies(pairs, sems):
    made = [pltpu.make_async_copy(a, b, sems.at[n]) for n, (a, b) in enumerate(pairs)]
    for copy in made:
        copy.start()
    return made


def finished(made):
    for copy in made:
        copy.wait()


def into_blocks(part_refs, blocks_ref):
    each = part_refs[0].shape[-1] // LANES
    return [
        (part.at[:, pl.ds(b * LANES, LANES)], blocks_ref.at[n * each + b])
        for n, part in enumerate(part_refs)
        for b in range(each)
    ]


def operated(blocks_ref, g_ref, pattern_ref, me, coefs, c, relative):
    total = None
    own = g_ref.shape[1]
    for k in range(g_ref.shape[0]):
        rows = []
        for t in range(g_ref.shape[2]):
            row = pattern_ref[k, t, me * own + c]
            if relative:
                owner = lax.div(row, own)
                row = (owner ^ me) * own + lax.rem(row, own)
            rows.append(blocks_ref[row])
        weights = g_ref[k, c].reshape(-1, LANES)
        product = jnp.dot(jnp.concatenate(rows, axis=1), weights, preferred_element_type=F32)
        scaled = coefs[k] * product
        total = scaled if total is None else total + scaled
    return total


def columns_of(coef, count):
    return [coef[:, k : k + 1] for k in range(count)]


def lanes_of(c):
    return pl.ds(pl.multiple_of(c * LANES, LANES), LANES)


def bulk_kernel(skip, me_ref, pattern_ref, a_ref, b_ref, c_ref, d_ref, g_ref, coef_ref, out_ref, blocks_ref, sems):
    made = copies(into_blocks([a_ref, b_ref, c_ref, d_ref], blocks_ref), sems)
    coefs = columns_of(coef_ref[skip : skip + out_ref.shape[0]], g_ref.shape[0])
    finished(made)

    @pl.loop(0, g_ref.shape[1])
    def _(c):
        out_ref[:, lanes_of(c)] = operated(blocks_ref, g_ref, pattern_ref, me_ref[0], coefs, c, True)


def bulk(me, pattern, parts, gblocks, coef, skip):
    rows, modes = parts[0].shape
    return pl.pallas_call(
        functools.partial(bulk_kernel, skip),
        in_specs=[SMEM, SMEM] + [ANY] * 4 + [VMEM] * 2,
        out_specs=VMEM,
        out_shape=shape((rows, modes)),
        scratch_shapes=[
            pltpu.VMEM((4 * modes // LANES, rows, LANES), BF16),
            pltpu.SemaphoreType.DMA((16,)),
        ],
        compiler_params=params(16),
    )(me, pattern, *parts, gblocks, coef)


def two_terms(value):
    high = value.astype(BF16).astype(F32)
    return high, value - high


def feed_of(rows, inverse):
    coarse = inverse.shape[0]
    inverse_t = jnp.transpose(inverse)
    feed = inverse_t[:, :1] * rows[:1]
    for c in range(1, coarse):
        feed = feed + inverse_t[:, c : c + 1] * rows[c : c + 1]
    return feed


def flags(index_ref, node):
    coarse = index_ref.shape[0]
    row = lax.broadcasted_iota(jnp.int32, (coarse, LANES), 0)
    found = jnp.zeros((coarse, LANES), F32)
    for c in range(coarse):
        found = jnp.where((row == c) & (index_ref[c] == node), 1.0, found)
    return found


def folded(row):
    count = row.shape[1] // LANES
    return jnp.concatenate([row[:, b * LANES : (b + 1) * LANES] for b in range(count)], axis=0)


def unfolded(rows):
    return jnp.concatenate([rows[b : b + 1] for b in range(rows.shape[0])], axis=1)


LAST, FIRST, NEXT = 32, 33, 48


def first_kernel(me_ref, pattern_ref, index_ref, a_ref, b_ref, c_ref, d_ref, g_ref, coef_ref, right_ref, mid_ref, sub_ref, field_ref, inverse_ref, coupling_ref, message_ref, base_ref, diffs_ref, around_ref, blocks_ref, res_ref, sub_vmem, base_vmem, diffs_vmem, rows_ref, sems):
    nodes, _ = field_ref.shape
    coarse = inverse_ref.shape[0]
    made = copies(
        into_blocks([a_ref, b_ref, c_ref, d_ref], blocks_ref)
        + [(right_ref, res_ref), (sub_ref, sub_vmem), (field_ref, base_vmem)],
        sems,
    )
    coef = jnp.concatenate([coef_ref[:EDGE], coef_ref[nodes - EDGE :]], axis=0)
    coefs = columns_of(coef, g_ref.shape[0])
    finished(made[:17])
    inner = slice(EDGE, nodes - EDGE)
    res_ref[inner] = res_ref[inner] - mid_ref[...]

    @pl.loop(0, g_ref.shape[1])
    def _(c):
        total = operated(blocks_ref, g_ref, pattern_ref, me_ref[0], coefs, c, True)
        res_ref[:EDGE, lanes_of(c)] = res_ref[:EDGE, lanes_of(c)] - total[:EDGE]
        res_ref[nodes - EDGE :, lanes_of(c)] = res_ref[nodes - EDGE :, lanes_of(c)] - total[EDGE:]

    finished(made[17:])
    for c in range(coarse):
        rows_ref[c : c + 1] = res_ref[pl.ds(index_ref[c], 1), :]
    feed = feed_of(rows_ref[...], inverse_ref[...])
    local = jnp.dot(sub_vmem[...], res_ref[...].astype(BF16), preferred_element_type=F32)
    base = base_vmem[...] + local
    base_vmem[...] = base
    out = [pltpu.make_async_copy(base_vmem, base_ref, sems.at[0])]
    out[0].start()
    diffs = 2.0 * base - pltpu.roll(base, 1, 0) - pltpu.roll(base, nodes - 1, 0)
    diffs_vmem[...] = diffs.astype(BF16)
    out.append(pltpu.make_async_copy(diffs_vmem, diffs_ref, sems.at[1]))
    out[1].start()

    lane = lax.broadcasted_iota(jnp.int32, (coarse, LANES), 1)
    high, low = two_terms(
        jnp.concatenate([jnp.transpose(coupling_ref[...]), jnp.zeros((coarse, LANES - coarse), F32)], axis=1)
    )
    at_last, at_first = flags(index_ref, nodes - 1), flags(index_ref, 0)
    block = high + pltpu.roll(low, coarse, 1)
    block = block + jnp.where(lane == LAST, at_last, 0.0) + jnp.where(lane == FIRST, at_first, 0.0)
    first = base[:1] + jnp.sum(at_first[:, :1] * feed.astype(BF16).astype(F32), axis=0, keepdims=True)
    edge = jnp.concatenate(
        two_terms(folded(base[nodes - 1 :])) + two_terms(folded(first)), axis=0
    )
    sent = jnp.concatenate([feed, block, edge], axis=1).astype(BF16)
    for p in range(message_ref.shape[0]):
        message_ref[p] = sent
    for j, n in enumerate(around(index_ref, nodes)):
        around_ref[j : j + 1] = base_vmem[at(n), :]
    finished(out)


def first_update(me, pattern, index, parts, gblocks, coef, right, mid, sub_t, field, inverse, coupling, plane):
    nodes, modes = right.shape
    coarse = inverse.shape[0]
    return pl.pallas_call(
        first_kernel,
        in_specs=[SMEM] * 3 + [ANY] * 4 + [VMEM] * 2 + [ANY, VMEM] + [ANY] * 2 + [VMEM] * 2,
        out_specs=[VMEM, ANY, ANY, VMEM],
        out_shape=[
            shape((plane, coarse, modes + 2 * LANES), BF16),
            shape((nodes, modes)),
            shape((nodes, modes), BF16),
            shape((padded(5 * coarse + 4), modes)),
        ],
        scratch_shapes=[
            pltpu.VMEM((4 * modes // LANES, 2 * EDGE, LANES), BF16),
            pltpu.VMEM((nodes, modes), F32),
            pltpu.VMEM((nodes, nodes), BF16),
            pltpu.VMEM((nodes, modes), F32),
            pltpu.VMEM((nodes, modes), BF16),
            pltpu.VMEM((coarse, modes), F32),
            pltpu.SemaphoreType.DMA((19,)),
        ],
        compiler_params=params(24),
        name="first_update",
    )(me, pattern, index, *parts, gblocks, coef, right, mid, sub_t, field, inverse, coupling)


def advance(coupling_t, state, push):
    moved = push
    for c in range(state.shape[0]):
        moved = moved + coupling_t[:, c : c + 1] * state[c : c + 1]
    return moved


def step_of(block, coarse, at=0):
    block = block.astype(F32)
    if at:
        block = pltpu.roll(block, LANES - at, 1)
    return block + pltpu.roll(block, LANES - coarse, 1)


def plane_kernel(feeds_ref, out_ref):
    plane, coarse, width = feeds_ref.shape
    modes = width - 2 * LANES
    row = lax.broadcasted_iota(jnp.int32, (coarse, LANES), 0)
    lane = lax.broadcasted_iota(jnp.int32, (coarse, LANES), 1)
    matrix = (row == lane).astype(F32)
    state = jnp.zeros((coarse, modes), F32)
    for p in range(plane):
        step = step_of(feeds_ref[p, :, modes : modes + LANES], coarse)
        state = advance(step, state, feeds_ref[p, :, :modes].astype(F32))
        matrix = advance(step, matrix, jnp.zeros_like(matrix))
    matrix = jnp.where(lane < coarse, matrix, 0.0)
    high, low = two_terms(matrix)
    first = feeds_ref[0, :, modes : modes + LANES].astype(F32)
    final = feeds_ref[plane - 1, :, modes : modes + LANES].astype(F32)
    block = high + pltpu.roll(low, coarse, 1)
    block = block + jnp.where(lane == LAST, final, 0.0) + jnp.where(lane == FIRST, first, 0.0)
    block = block + jnp.where((lane >= NEXT) & (lane < NEXT + 2 * coarse), pltpu.roll(first, NEXT, 1), 0.0)
    edge = jnp.where(
        row < coarse // 2,
        feeds_ref[plane - 1, :, modes + LANES :].astype(F32),
        feeds_ref[0, :, modes + LANES :].astype(F32),
    )
    sent = jnp.concatenate([state, block, edge], axis=1).astype(BF16)
    for z in range(out_ref.shape[0]):
        out_ref[z] = sent


def plane_totals(feeds, planes):
    _, coarse, width = feeds.shape
    return pl.pallas_call(
        plane_kernel,
        in_specs=[VMEM],
        out_specs=VMEM,
        out_shape=shape((planes, coarse, width), BF16),
        compiler_params=params(8),
        name="plane_totals",
    )(feeds)


def second_plane_kernel(feeds_ref, first_ref, out_ref):
    plane, coarse, modes = feeds_ref.shape
    state = feeds_ref[0].astype(F32)
    for p in range(1, plane):
        step = step_of(first_ref[p, :, modes : modes + LANES], coarse)
        state = advance(step, state, feeds_ref[p].astype(F32))
    for z in range(out_ref.shape[0]):
        out_ref[z] = state.astype(BF16)


def second_plane_totals(feeds, first, planes):
    _, coarse, modes = feeds.shape
    return pl.pallas_call(
        second_plane_kernel,
        in_specs=[VMEM] * 2,
        out_specs=VMEM,
        out_shape=shape((planes, coarse, modes), BF16),
        compiler_params=params(8),
        name="second_plane_totals",
    )(feeds, first)


def errors(z_ref, p_ref, feeds_ref, totals_ref, steps_ref, plane_steps_ref):
    coarse = steps_ref.shape[1]
    modes = steps_ref.shape[2] - 2 * LANES

    def across(z, state):
        step = step_of(plane_steps_ref[z, :, modes : modes + LANES], coarse)
        return advance(step, state, totals_ref[z, :, :modes].astype(F32))

    def within(p, state):
        step = step_of(steps_ref[p, :, modes : modes + LANES], coarse)
        return advance(step, state, feeds_ref[p, :, :modes].astype(F32))

    before = lax.fori_loop(0, z_ref[0], across, jnp.zeros((coarse, modes), F32))
    before = lax.fori_loop(0, p_ref[0], within, before)
    return before, within(p_ref[0], before)


def correct_kernel(z_ref, p_ref, index_ref, feeds_ref, totals_ref, around_ref, sent_ref, error_ref, wide_ref, rows_ref):
    nodes, modes = wide_ref.shape[0] - 16, wide_ref.shape[1]
    plane, planes = feeds_ref.shape[0], totals_ref.shape[0]
    z, p = z_ref[0], p_ref[0]
    before, error = errors(z_ref, p_ref, feeds_ref, totals_ref, feeds_ref, totals_ref)
    coarse = error.shape[0]

    block, edge = slice(modes, modes + LANES), slice(modes + LANES, modes + 2 * LANES)
    p_left, z_left = jnp.maximum(p - 1, 0), jnp.maximum(z - 1, 0)
    p_right, z_right = jnp.minimum(p + 1, plane - 1), jnp.minimum(z + 1, planes - 1)
    here = p > 0
    left_block = jnp.where(here, feeds_ref[p_left, :, block].astype(F32), totals_ref[z_left, :, block].astype(F32))
    left_edge = jnp.where(here, feeds_ref[p_left, :, edge].astype(F32), totals_ref[z_left, :, edge].astype(F32))
    left = unfolded(left_edge[:4] + left_edge[4:8])
    left = left + jnp.sum(left_block[:, LAST : LAST + 1] * before, axis=0, keepdims=True)
    left = jnp.where((z > 0) | here, left, 0.0)
    here = p < plane - 1
    near, far = feeds_ref[p_right, :, block], totals_ref[z_right, :, block]
    step = jnp.where(here, step_of(near, coarse), step_of(far, coarse, NEXT))
    flag = jnp.where(here, near.astype(F32), far.astype(F32))
    right_edge = jnp.where(here, feeds_ref[p_right, :, edge].astype(F32), totals_ref[z_right, :, edge].astype(F32))
    moved = advance(step, error, jnp.zeros_like(error))
    right = unfolded(right_edge[8:12] + right_edge[12:])
    right = right + jnp.sum(flag[:, FIRST : FIRST + 1] * moved, axis=0, keepdims=True)
    right = jnp.where((z < planes - 1) | here, right, 0.0)

    error_ref[...] = error
    for j, n in enumerate(around(index_ref, nodes)):
        wide_ref[at(8 + n), :] = around_ref[j : j + 1]
    wide_ref[7:8] = left
    wide_ref[8 + nodes : 9 + nodes] = right
    for c in range(coarse):
        row = pl.ds(8 + index_ref[c], 1)
        wide_ref[row, :] = wide_ref[row, :] + error[c : c + 1]
    found = affected(index_ref, nodes)
    rows_ref[...] = jnp.zeros_like(rows_ref)
    for j, n in enumerate(found):
        rows_ref[j : j + 1] = (
            2.0 * wide_ref[at(8 + n), :] - wide_ref[at(7 + n), :] - wide_ref[at(9 + n), :]
        )
    sent = rows_ref[...].astype(BF16)
    for m in range(sent_ref.shape[0]):
        sent_ref[m] = sent


def correct(z, p, index, feeds, totals, near, nodes, modes_by):
    modes = near.shape[1]
    coarse = index.shape[0]
    rows = padded(3 * coarse + 2)
    return pl.pallas_call(
        correct_kernel,
        in_specs=[SMEM] * 3 + [VMEM] * 3,
        out_specs=[VMEM] * 2,
        out_shape=[shape((modes_by, rows, modes), BF16), shape((coarse, modes))],
        scratch_shapes=[pltpu.VMEM((nodes + 16, modes), F32), pltpu.VMEM((rows, modes), F32)],
        compiler_params=params(16),
        name="correct",
    )(z, p, index, feeds, totals, near)


def redo_kernel(me_ref, pattern_ref, diffs_ref, g_ref, coef_ref, right_ref, inverse_ref, message_ref, res_ref, blocks_ref, rows_ref, sems):
    made = copies(into_blocks([diffs_ref.at[m] for m in range(diffs_ref.shape[0])], blocks_ref), sems)
    coefs = columns_of(coef_ref[...], g_ref.shape[0])
    finished(made)

    @pl.loop(0, g_ref.shape[1])
    def _(c):
        total = operated(blocks_ref, g_ref, pattern_ref, me_ref[0], coefs, c, False)
        res_ref[:, lanes_of(c)] = right_ref[:, lanes_of(c)] - total

    for c in range(inverse_ref.shape[0]):
        rows_ref[c : c + 1] = res_ref[3 * c + 1 : 3 * c + 2]
    feed = feed_of(rows_ref[...], inverse_ref[...]).astype(BF16)
    for p in range(message_ref.shape[0]):
        message_ref[p] = feed


def redo(me, pattern, diffs, gblocks, coef_rows, right_rows, inverse, plane):
    rows, modes = right_rows.shape
    coarse = inverse.shape[0]
    return pl.pallas_call(
        redo_kernel,
        in_specs=[SMEM] * 2 + [ANY] + [VMEM] * 4,
        out_specs=[VMEM] * 2,
        out_shape=[shape((plane, coarse, modes), BF16), shape((rows, modes))],
        scratch_shapes=[
            pltpu.VMEM((4 * modes // LANES, rows, LANES), BF16),
            pltpu.VMEM((coarse, modes), F32),
            pltpu.SemaphoreType.DMA((16,)),
        ],
        compiler_params=params(16),
        name="redo",
    )(me, pattern, diffs, gblocks, coef_rows, right_rows, inverse)


def last_local_kernel(index_ref, op_ref, right_ref, rows_ref, sub_ref, base_ref, error_ref, base_out_ref, res_out_ref, res_ref, field_ref):
    nodes = op_ref.shape[0]
    res_ref[...] = right_ref[...] - op_ref[...]
    for j, n in enumerate(affected(index_ref, nodes)):
        res_ref[at(n), :] = rows_ref[j : j + 1]
    res = res_ref[...]
    field_ref[...] = base_ref[...] + jnp.dot(sub_ref[...], res.astype(BF16), preferred_element_type=F32)
    for c in range(error_ref.shape[0]):
        field_ref[at(index_ref[c]), :] = field_ref[at(index_ref[c]), :] + error_ref[c : c + 1]
    base_out_ref[...] = jnp.transpose(field_ref[...])
    res_out_ref[...] = jnp.transpose(res)


def last_local(index, op, right, rows, sub_t, base, error):
    nodes, modes = op.shape
    column = lambda height: pl.BlockSpec((height, LANES), lambda j: (0, j))
    row = pl.BlockSpec((LANES, nodes), lambda j: (j, 0))
    return pl.pallas_call(
        last_local_kernel,
        grid=(modes // LANES,),
        in_specs=[
            SMEM,
            column(nodes),
            column(nodes),
            column(rows.shape[0]),
            pl.BlockSpec((nodes, nodes), lambda j: (0, 0)),
            column(nodes),
            column(error.shape[0]),
        ],
        out_specs=[row, row],
        out_shape=[shape((modes, nodes)), shape((modes, nodes))],
        scratch_shapes=[pltpu.VMEM((nodes, LANES), F32), pltpu.VMEM((nodes, LANES), F32)],
        name="last_local",
    )(index, op, right, rows, sub_t, base, error)


def last_kernel(z_ref, p_ref, index_ref, feeds_ref, totals_ref, steps_ref, plane_steps_ref, base_ref, out_ref, base_vmem, out_vmem, sems):
    modes, nodes = base_ref.shape
    load = pltpu.make_async_copy(base_ref, base_vmem, sems.at[0])
    load.start()
    _, error = errors(z_ref, p_ref, feeds_ref, totals_ref, steps_ref, plane_steps_ref)
    coarse = error.shape[0]
    high = error.astype(BF16).astype(F32)
    rest = error - high
    mid = rest.astype(BF16).astype(F32)
    terms = jnp.transpose(jnp.concatenate([high, mid, rest - mid], axis=0)).astype(BF16)
    node = lax.broadcasted_iota(jnp.int32, (coarse, nodes), 1)
    row = lax.broadcasted_iota(jnp.int32, (coarse, nodes), 0)
    wanted = jnp.zeros((coarse, nodes), jnp.int32)
    for c in range(coarse):
        wanted = jnp.where(row == c, index_ref[c], wanted)
    onehot = (node == wanted).astype(F32)
    onehot = jnp.concatenate([onehot] * 3, axis=0).astype(BF16)
    load.wait()
    made = []
    for n in range(modes // LANES):
        rows = slice(n * LANES, (n + 1) * LANES)
        out_vmem[rows] = base_vmem[rows] + jnp.dot(terms[rows], onehot, preferred_element_type=F32)
        made.append(pltpu.make_async_copy(out_vmem.at[rows], out_ref.at[rows], sems.at[1 + n]))
        made[-1].start()
    finished(made)


def last(z, p, index, feeds, totals, steps, plane_steps, base):
    modes, _ = base.shape
    return pl.pallas_call(
        last_kernel,
        in_specs=[SMEM] * 3 + [VMEM] * 4 + [ANY],
        out_specs=ANY,
        out_shape=shape(base.shape),
        scratch_shapes=[
            pltpu.VMEM(base.shape, F32),
            pltpu.VMEM(base.shape, F32),
            pltpu.SemaphoreType.DMA((1 + modes // LANES,)),
        ],
        compiler_params=params(16),
        name="last",
    )(z, p, index, feeds, totals, steps, plane_steps, base)


def from_neighbours(last_rows, first_rows):
    size = lax.axis_size(SUB)
    up = [(i, i + 1) for i in range(size - 1)]
    left = lax.ppermute(last_rows, SUB, up)
    right = lax.ppermute(first_rows, SUB, [(j, i) for i, j in up])
    return left, right


def over_modes(own):
    swap = [(0, 1), (1, 0)]
    across = lax.ppermute(own, "yl", swap)
    beside = lax.ppermute(own, "core", swap)
    onward = lax.ppermute(across, "core", swap)
    return own, beside, across, onward


def shards(right_side, start_field, coefficient, gblocks, pattern, sub_inverse, coarse_index, coarse_inv, coupling):
    me = lax.axis_index(MODE).reshape(1)
    z, p = lax.axis_index("z").reshape(1), lax.axis_index(PLANE).reshape(1)
    planes, plane = lax.axis_size("z"), lax.axis_size(PLANE)
    nodes = start_field.shape[1]
    pattern = jnp.swapaxes(pattern, 1, 2)
    diffs, top, low, last_rows, first_rows = start(start_field)
    parts = over_modes(diffs)
    left, right = from_neighbours(last_rows, first_rows)
    edge_rows = edges(top, low, left, right)
    edge_parts = over_modes(edge_rows)
    rhs, sub_t, field, coef, right_rows, coef_rows = prepare(
        coarse_index, right_side, sub_inverse, start_field, coefficient
    )
    mid = bulk(me, pattern, parts, gblocks, coef, EDGE)
    message, base, diffs, near = first_update(
        me, pattern, coarse_index, edge_parts, gblocks, coef, rhs, mid, sub_t, field, coarse_inv, coupling, plane
    )
    feeds = lax.all_to_all(message, PLANE, 0, 0, tiled=True)
    diffs, feeds = lax.optimization_barrier((diffs, feeds))
    parts = over_modes(diffs)
    totals = plane_totals(feeds, planes)
    totals = lax.all_to_all(totals, "z", 0, 0, tiled=True)
    rows, error = correct(z, p, coarse_index, feeds, totals, near, nodes, lax.axis_size(MODE))
    rows = lax.all_to_all(rows, MODE, 0, 0, tiled=True)
    op = bulk(me, pattern, parts, gblocks, coef, 0)
    message, res_rows = redo(me, pattern, rows, gblocks, coef_rows, right_rows, coarse_inv, plane)
    later = lax.all_to_all(message, PLANE, 0, 0, tiled=True)
    base, residual = last_local(coarse_index, op, rhs, res_rows, sub_t, base, error)
    later_totals = second_plane_totals(later, feeds, planes)
    later_totals = lax.all_to_all(later_totals, "z", 0, 0, tiled=True)
    field = last(z, p, coarse_index, later, later_totals, feeds, totals, base)
    return field, residual


def solution(mesh):
    split = Mesh(mesh.devices.reshape(8, 4, 2, 2, 2), SUB + MODE)
    placed = (
        P(MODE, SUB),
        P(MODE, SUB),
        P(None, SUB),
        P(None, MODE, None, None, None),
        P(),
        P(SUB, None),
        P(SUB),
        P(SUB, None),
        P(SUB, None),
    )
    return jax.shard_map(shards, mesh=split, in_specs=placed, out_specs=(P(MODE, SUB), P(MODE, SUB)), check_vma=False)
```

```python
import jax
import jax.numpy as jnp
from jax import lax
from jax.experimental import pallas as pl
from jax.experimental.pallas import tpu as pltpu
from jax.sharding import Mesh
from jax.sharding import PartitionSpec as P

SUB = ("z", "x", "yh")
PLANE = ("x", "yh")
MODE = ("yl", "core")
EDGE = 16
LANES = 128
F32 = jnp.float32
BF16 = jnp.bfloat16
VMEM = pl.BlockSpec(memory_space=pltpu.VMEM)
SMEM = pl.BlockSpec(memory_space=pltpu.SMEM)


def params(kib=63600):
    return pltpu.CompilerParams(vmem_limit_bytes=kib * 1024)


def shape(dims, dtype=F32):
    return jax.ShapeDtypeStruct(dims, dtype)


def start_kernel(field_ref, middle_ref, top_ref, low_ref, last_ref, first_ref):
    field = jnp.transpose(field_ref[...])
    nodes = field.shape[0]
    diffs = 2.0 * field - pltpu.roll(field, 1, 0) - pltpu.roll(field, nodes - 1, 0)
    middle_ref[...] = diffs[EDGE : nodes - EDGE].astype(BF16)
    top_ref[...] = field[: EDGE + 8]
    low_ref[...] = field[nodes - EDGE - 8 :]
    last_ref[...] = jnp.broadcast_to(field[nodes - 1 :], last_ref.shape)
    first_ref[...] = jnp.broadcast_to(field[:1], first_ref.shape)


def start(field):
    modes, nodes = field.shape
    column = lambda rows: pl.BlockSpec((rows, LANES), lambda j: (0, j))
    return pl.pallas_call(
        start_kernel,
        grid=(modes // LANES,),
        in_specs=[pl.BlockSpec((LANES, nodes), lambda j: (j, 0))],
        out_specs=[column(nodes - 2 * EDGE), column(EDGE + 8), column(EDGE + 8), column(8), column(8)],
        out_shape=[
            shape((nodes - 2 * EDGE, modes), BF16),
            shape((EDGE + 8, modes)),
            shape((EDGE + 8, modes)),
            shape((8, modes)),
            shape((8, modes)),
        ],
        name="start",
    )(field)


def affected(index_ref, nodes):
    found = []
    for c in range(index_ref.shape[0]):
        for off in (-1, 0, 1):
            found.append(jnp.clip(index_ref[c] + off, 0, nodes - 1))
    return found + [0, nodes - 1]


def around(index_ref, nodes):
    found = []
    for c in range(index_ref.shape[0]):
        for off in (-2, -1, 0, 1, 2):
            found.append(jnp.clip(index_ref[c] + off, 0, nodes - 1))
    return found + [0, 1, nodes - 2, nodes - 1]


def padded(count):
    return -(-count // 16) * 16


def at(row):
    return slice(row, row + 1) if isinstance(row, int) else pl.ds(row, 1)


def prepare_kernel(index_ref, right_ref, inverse_ref, field_ref, coef_ref, right_t_ref, inverse_t_ref, field_t_ref, coef_t_ref, right_rows_ref, coef_rows_ref):
    right_t_ref[...] = jnp.transpose(right_ref[...])
    inverse_t_ref[...] = jnp.transpose(inverse_ref[...].astype(F32)).astype(BF16)
    field_t_ref[...] = jnp.transpose(field_ref[...])
    terms, nodes = coef_ref.shape
    found = affected(index_ref, nodes)
    right_rows_ref[...] = jnp.zeros_like(right_rows_ref)
    for j, n in enumerate(found):
        right_rows_ref[j : j + 1] = right_t_ref[at(n), :]

    @pl.when(pl.program_id(0) == 0)
    def _():
        wide = jnp.concatenate([coef_ref[...], jnp.zeros((LANES - terms, nodes), F32)], axis=0)
        coef_t_ref[...] = jnp.transpose(wide)
        coef_rows_ref[...] = jnp.zeros_like(coef_rows_ref)
        for j, n in enumerate(found):
            coef_rows_ref[j : j + 1] = coef_t_ref[at(n), :]


def prepare(index, right_side, sub_inverse, field, coefficient):
    modes, nodes = right_side.shape
    count = padded(3 * index.shape[0] + 2)
    rows = lambda width: pl.BlockSpec((LANES, width), lambda j: (j, 0))
    column = lambda height: pl.BlockSpec((height, LANES), lambda j: (0, j))
    fixed = lambda height: pl.BlockSpec((height, LANES), lambda j: (0, 0))
    return pl.pallas_call(
        prepare_kernel,
        grid=(modes // LANES,),
        in_specs=[
            SMEM,
            rows(nodes),
            rows(nodes),
            rows(nodes),
            pl.BlockSpec(coefficient.shape, lambda j: (0, 0)),
        ],
        out_specs=[column(nodes)] * 3 + [fixed(nodes), column(count), fixed(count)],
        out_shape=[
            shape((nodes, modes)),
            shape((nodes, nodes), BF16),
            shape((nodes, modes)),
            shape((nodes, LANES)),
            shape((count, modes)),
            shape((count, LANES)),
        ],
        name="prepare",
    )(index, right_side, sub_inverse, field, coefficient)


def edge_kernel(top_ref, low_ref, left_ref, right_ref, edge_ref):
    top = top_ref[...]
    before = jnp.concatenate([left_ref[:1], top[: EDGE - 1]], axis=0)
    edge_ref[:EDGE] = (2.0 * top[:EDGE] - before - top[1 : EDGE + 1]).astype(BF16)
    low = low_ref[...]
    after = jnp.concatenate([low[9:], right_ref[:1]], axis=0)
    edge_ref[EDGE:] = (2.0 * low[8:] - low[7:-1] - after).astype(BF16)


def edges(top, low, left, right):
    return pl.pallas_call(
        edge_kernel,
        in_specs=[VMEM] * 4,
        out_specs=VMEM,
        out_shape=shape((2 * EDGE, top.shape[1]), BF16),
        compiler_params=params(16384),
        name="edges",
    )(top, low, left, right)


HBM = pl.BlockSpec(memory_space=pltpu.HBM)
ANY = pl.BlockSpec(memory_space=pl.ANY)


def copies(pairs, sems):
    made = [pltpu.make_async_copy(a, b, sems.at[n]) for n, (a, b) in enumerate(pairs)]
    for copy in made:
        copy.start()
    return made


def finished(made):
    for copy in made:
        copy.wait()


def into_blocks(part_refs, blocks_ref, rows=slice(None)):
    each = part_refs[0].shape[-1] // LANES
    return [
        (part.at[:, pl.ds(b * LANES, LANES)], blocks_ref.at[n * each + b, rows])
        for n, part in enumerate(part_refs)
        for b in range(each)
    ]


def operated(blocks_ref, g_ref, pattern_ref, me, first, coefs, c):
    total = None
    own = pattern_ref.shape[2] // 4
    for k in range(g_ref.shape[0]):
        rows = []
        for t in range(g_ref.shape[2]):
            row = pattern_ref[k, t, me * own + first + c]
            owner = lax.div(row, own)
            row = (owner ^ me) * own + lax.rem(row, own)
            rows.append(blocks_ref[row])
        weights = g_ref[k, c].reshape(-1, LANES)
        product = jnp.dot(jnp.concatenate(rows, axis=1), weights, preferred_element_type=F32)
        scaled = coefs[k] * product
        total = scaled if total is None else total + scaled
    return total


def weights_into(g_ref, g_vmem, sems, first):
    return [
        pltpu.make_async_copy(g_ref.at[:, c], g_vmem.at[:, c], sems.at[first + c])
        for c in range(g_ref.shape[1])
    ]


def wait_weights(g_ref, g_vmem, sems, first, c):
    pltpu.make_async_copy(g_ref.at[:, c], g_vmem.at[:, c], sems.at[first + c]).wait()


def columns_of(coef, count):
    return [coef[:, k : k + 1] for k in range(count)]


def lanes_of(c):
    return pl.ds(pl.multiple_of(c * LANES, LANES), LANES)


def bulk_kernel(me_ref, pattern_ref, a_ref, b_ref, c_ref, d_ref, g_hbm, coef_ref, out_ref, blocks_ref, g_ref, sems):
    weights = weights_into(g_hbm, g_ref, sems, 16)
    weights[0].start()
    made = copies(into_blocks([a_ref, b_ref, c_ref, d_ref], blocks_ref), sems)
    for copy in weights[1:]:
        copy.start()
    coefs = columns_of(coef_ref[...], g_ref.shape[0])
    finished(made)

    @pl.loop(0, g_ref.shape[1])
    def _(c):
        wait_weights(g_hbm, g_ref, sems, 16, c)
        out_ref[:, lanes_of(c)] = operated(blocks_ref, g_ref, pattern_ref, me_ref[0], 0, coefs, c)


def bulk(me, pattern, parts, gblocks, coef):
    rows, modes = parts[0].shape
    return pl.pallas_call(
        bulk_kernel,
        in_specs=[SMEM, SMEM] + [ANY] * 5 + [VMEM],
        out_specs=VMEM,
        out_shape=shape((rows, modes)),
        scratch_shapes=[
            pltpu.VMEM((4 * modes // LANES, rows, LANES), BF16),
            pltpu.VMEM(gblocks.shape, BF16),
            pltpu.SemaphoreType.DMA((16 + gblocks.shape[1],)),
        ],
        compiler_params=params(52000),
        name="whole",
    )(me, pattern, *parts, gblocks, coef)


def hold_kernel(g_ref, after_ref, out_ref, sems):
    del after_ref
    made = [
        pltpu.make_async_copy(g_ref.at[:, c], out_ref.at[:, c], sems.at[c])
        for c in range(out_ref.shape[1])
    ]
    for copy in made:
        copy.start()
    finished(made)


def hold(gblocks, after, count):
    terms, _, *rest = gblocks.shape
    return pl.pallas_call(
        hold_kernel,
        in_specs=[HBM, ANY],
        out_specs=VMEM,
        out_shape=shape((terms, count, *rest), BF16),
        scratch_shapes=[pltpu.SemaphoreType.DMA((count,))],
        compiler_params=params(16384),
    )(gblocks, after)


def two_terms(value):
    high = value.astype(BF16).astype(F32)
    return high, value - high


def feed_of(rows, inverse):
    coarse = inverse.shape[0]
    inverse_t = jnp.transpose(inverse)
    feed = inverse_t[:, :1] * rows[:1]
    for c in range(1, coarse):
        feed = feed + inverse_t[:, c : c + 1] * rows[c : c + 1]
    return feed


def flags(index_ref, node):
    coarse = index_ref.shape[0]
    row = lax.broadcasted_iota(jnp.int32, (coarse, LANES), 0)
    found = jnp.zeros((coarse, LANES), F32)
    for c in range(coarse):
        found = jnp.where((row == c) & (index_ref[c] == node), 1.0, found)
    return found


def folded(row):
    count = row.shape[1] // LANES
    return jnp.concatenate([row[:, b * LANES : (b + 1) * LANES] for b in range(count)], axis=0)


def unfolded(rows):
    return jnp.concatenate([rows[b : b + 1] for b in range(rows.shape[0])], axis=1)


LAST, FIRST, NEXT = 32, 33, 48


def first_kernel(me_ref, pattern_ref, index_ref, a_ref, b_ref, c_ref, d_ref, ea_ref, eb_ref, ec_ref, ed_ref, g_hbm, coef_ref, right_ref, sub_ref, field_ref, inverse_ref, coupling_ref, message_ref, base_ref, diffs_ref, around_ref, blocks_ref, res_ref, sub_vmem, base_vmem, diffs_vmem, rows_ref, g_ref, sems):
    nodes, _ = field_ref.shape
    coarse = inverse_ref.shape[0]
    inner = pl.ds(EDGE, nodes - 2 * EDGE)
    weights = weights_into(g_hbm, g_ref, sems, 51)
    weights[0].start()
    made = copies(
        into_blocks([a_ref, b_ref, c_ref, d_ref], blocks_ref, inner)
        + into_blocks([r.at[pl.ds(0, EDGE)] for r in (ea_ref, eb_ref, ec_ref, ed_ref)], blocks_ref, pl.ds(0, EDGE))
        + into_blocks([r.at[pl.ds(EDGE, EDGE)] for r in (ea_ref, eb_ref, ec_ref, ed_ref)], blocks_ref, pl.ds(nodes - EDGE, EDGE))
        + [(right_ref, res_ref)],
        sems,
    )
    for copy in weights[1:]:
        copy.start()
    later = [
        pltpu.make_async_copy(sub_ref, sub_vmem, sems.at[49]),
        pltpu.make_async_copy(field_ref, base_vmem, sems.at[50]),
    ]
    for copy in later:
        copy.start()
    coefs = columns_of(coef_ref[...], g_ref.shape[0])
    finished(made)

    @pl.loop(0, g_ref.shape[1])
    def _(c):
        wait_weights(g_hbm, g_ref, sems, 51, c)
        total = operated(blocks_ref, g_ref, pattern_ref, me_ref[0], 0, coefs, c)
        res_ref[:, lanes_of(c)] = res_ref[:, lanes_of(c)] - total

    finished(later)
    for c in range(coarse):
        rows_ref[c : c + 1] = res_ref[pl.ds(index_ref[c], 1), :]
    feed = feed_of(rows_ref[...], inverse_ref[...])
    local = jnp.dot(sub_vmem[...], res_ref[...].astype(BF16), preferred_element_type=F32)
    base = base_vmem[...] + local
    base_vmem[...] = base
    out = [pltpu.make_async_copy(base_vmem, base_ref, sems.at[0])]
    out[0].start()
    diffs = 2.0 * base - pltpu.roll(base, 1, 0) - pltpu.roll(base, nodes - 1, 0)
    diffs_vmem[...] = diffs.astype(BF16)
    out.append(pltpu.make_async_copy(diffs_vmem, diffs_ref, sems.at[1]))
    out[1].start()

    lane = lax.broadcasted_iota(jnp.int32, (coarse, LANES), 1)
    high, low = two_terms(
        jnp.concatenate([jnp.transpose(coupling_ref[...]), jnp.zeros((coarse, LANES - coarse), F32)], axis=1)
    )
    at_last, at_first = flags(index_ref, nodes - 1), flags(index_ref, 0)
    block = high + pltpu.roll(low, coarse, 1)
    block = block + jnp.where(lane == LAST, at_last, 0.0) + jnp.where(lane == FIRST, at_first, 0.0)
    first = base[:1] + jnp.sum(at_first[:, :1] * feed.astype(BF16).astype(F32), axis=0, keepdims=True)
    edge = jnp.concatenate(
        two_terms(folded(base[nodes - 1 :])) + two_terms(folded(first)), axis=0
    )
    sent = jnp.concatenate([feed, block, edge], axis=1).astype(BF16)
    for p in range(message_ref.shape[0]):
        message_ref[p] = sent
    for j, n in enumerate(around(index_ref, nodes)):
        around_ref[j : j + 1] = base_vmem[at(n), :]
    finished(out)


def first_update(me, pattern, index, parts, edge_parts, gblocks, coef, right, sub_t, field, inverse, coupling, plane):
    nodes, modes = right.shape
    coarse = inverse.shape[0]
    return pl.pallas_call(
        first_kernel,
        in_specs=[SMEM] * 3 + [ANY] * 9 + [VMEM] + [ANY] * 3 + [VMEM] * 2,
        out_specs=[VMEM, ANY, ANY, VMEM],
        out_shape=[
            shape((plane, coarse, modes + 2 * LANES), BF16),
            shape((nodes, modes)),
            shape((nodes, modes), BF16),
            shape((padded(5 * coarse + 4), modes)),
        ],
        scratch_shapes=[
            pltpu.VMEM((4 * modes // LANES, nodes, LANES), BF16),
            pltpu.VMEM((nodes, modes), F32),
            pltpu.VMEM((nodes, nodes), BF16),
            pltpu.VMEM((nodes, modes), F32),
            pltpu.VMEM((nodes, modes), BF16),
            pltpu.VMEM((coarse, modes), F32),
            pltpu.VMEM(gblocks.shape, BF16),
            pltpu.SemaphoreType.DMA((51 + gblocks.shape[1],)),
        ],
        compiler_params=params(52000),
        name="first_update",
    )(me, pattern, index, *parts, *edge_parts, gblocks, coef, right, sub_t, field, inverse, coupling)


def advance(coupling_t, state, push):
    moved = push
    for c in range(state.shape[0]):
        moved = moved + coupling_t[:, c : c + 1] * state[c : c + 1]
    return moved


def step_of(block, coarse, at=0):
    block = block.astype(F32)
    if at:
        block = pltpu.roll(block, LANES - at, 1)
    return block + pltpu.roll(block, LANES - coarse, 1)


def lanes_and_rows(coarse):
    row = lax.broadcasted_iota(jnp.int32, (coarse, LANES), 0)
    lane = lax.broadcasted_iota(jnp.int32, (coarse, LANES), 1)
    return row, lane


def side_by_side(squares):
    coarse = squares[0].shape[0]
    _, lane = lanes_and_rows(coarse)
    total = None
    for n, square in enumerate(squares):
        square = jnp.where(lane < coarse, square, 0.0)
        square = pltpu.roll(square, n * coarse, 1) if n else square
        total = square if total is None else total + square
    return total


def terms_of(weights):
    return jnp.concatenate(two_terms(weights), axis=0).astype(BF16)


def plane_kernel(p_ref, feeds_ref, out_ref, inside_ref, weights_ref, carry_ref):
    plane, coarse, width = feeds_ref.shape
    modes = width - 2 * LANES
    p = p_ref[0]
    row, lane = lanes_and_rows(coarse)
    one = (row == lane).astype(F32)
    none = jnp.zeros_like(one)
    whole, before = one, none
    wholes, befores = [], []
    for q in range(plane - 1, -1, -1):
        step = step_of(feeds_ref[q, :, modes : modes + LANES], coarse)
        before = jnp.where(q == p - 1, one, before)
        wholes.append(whole)
        befores.append(before)
        whole = advance(whole, step, none)
        before = advance(before, step, none)
    carry_ref[...] = jnp.where(p == 0, one, before)
    totals, excluding = side_by_side(wholes[::-1]), side_by_side(befores[::-1])
    own = step_of(feeds_ref[p, :, modes : modes + LANES], coarse)
    including = advance(own, excluding, (lane == p * coarse + row).astype(F32))
    totals = terms_of(totals)
    weights_ref[...] = jnp.concatenate([totals, terms_of(including)], axis=0)
    feeds = feeds_ref[:, :, :modes].reshape(plane * coarse, modes)
    sums = jnp.dot(jnp.concatenate([totals, terms_of(excluding)], axis=0), feeds, preferred_element_type=F32)
    state = sums[:coarse] + sums[coarse : 2 * coarse]
    inside_ref[...] = sums[2 * coarse : 3 * coarse] + sums[3 * coarse :]
    matrix = jnp.where(lane < coarse, whole, 0.0)
    high, low = two_terms(matrix)
    first = feeds_ref[0, :, modes : modes + LANES].astype(F32)
    final = feeds_ref[plane - 1, :, modes : modes + LANES].astype(F32)
    block = high + pltpu.roll(low, coarse, 1)
    block = block + jnp.where(lane == LAST, final, 0.0) + jnp.where(lane == FIRST, first, 0.0)
    block = block + jnp.where((lane >= NEXT) & (lane < NEXT + 2 * coarse), pltpu.roll(first, NEXT, 1), 0.0)
    edge = jnp.where(
        row < coarse // 2,
        feeds_ref[plane - 1, :, modes + LANES :].astype(F32),
        feeds_ref[0, :, modes + LANES :].astype(F32),
    )
    sent = jnp.concatenate([state, block, edge], axis=1).astype(BF16)
    for z in range(out_ref.shape[0]):
        out_ref[z] = sent


def plane_totals(p, feeds, planes):
    plane, coarse, width = feeds.shape
    return pl.pallas_call(
        plane_kernel,
        in_specs=[SMEM, VMEM],
        out_specs=[VMEM] * 4,
        out_shape=[
            shape((planes, coarse, width), BF16),
            shape((coarse, width - 2 * LANES)),
            shape((4 * coarse, plane * coarse), BF16),
            shape((coarse, LANES)),
        ],
        compiler_params=params(52000),
        name="plane_totals",
    )(p, feeds)


def second_plane_kernel(feeds_ref, weights_ref, out_ref, inside_ref):
    plane, coarse, modes = feeds_ref.shape
    feeds = feeds_ref[...].reshape(plane * coarse, modes)
    sums = jnp.dot(weights_ref[...], feeds, preferred_element_type=F32)
    state = (sums[:coarse] + sums[coarse : 2 * coarse]).astype(BF16)
    inside_ref[...] = sums[2 * coarse : 3 * coarse] + sums[3 * coarse :]
    for z in range(out_ref.shape[0]):
        out_ref[z] = state


def second_plane_totals(feeds, weights, planes):
    _, coarse, modes = feeds.shape
    return pl.pallas_call(
        second_plane_kernel,
        in_specs=[VMEM] * 2,
        out_specs=[VMEM] * 2,
        out_shape=[shape((planes, coarse, modes), BF16), shape((coarse, modes))],
        compiler_params=params(52000),
        name="second_plane_totals",
    )(feeds, weights)


def correct_kernel(z_ref, p_ref, index_ref, feeds_ref, totals_ref, inside_ref, carry_ref, around_ref, sent_ref, error_ref, weights_ref, wide_ref, rows_ref):
    nodes, modes = wide_ref.shape[0] - 16, wide_ref.shape[1]
    plane, planes = feeds_ref.shape[0], totals_ref.shape[0]
    z, p = z_ref[0], p_ref[0]
    coarse = index_ref.shape[0]
    none = jnp.zeros((coarse, LANES), F32)
    factor = none
    factors = []
    for q in range(planes - 1, -1, -1):
        factor = jnp.where(q == z - 1, carry_ref[...], factor)
        factors.append(factor)
        factor = advance(factor, step_of(totals_ref[q, :, modes : modes + LANES], coarse), none)
    weights = side_by_side(factors[::-1])
    totals = totals_ref[:, :, :modes].reshape(planes * coarse, modes)
    sums = jnp.dot(terms_of(weights), totals, preferred_element_type=F32)
    before = inside_ref[...] + sums[:coarse] + sums[coarse:]
    own = step_of(feeds_ref[p, :, modes : modes + LANES], coarse)
    error = advance(own, before, feeds_ref[p, :, :modes].astype(F32))
    weights_ref[...] = terms_of(advance(own, weights, none))

    block, edge = slice(modes, modes + LANES), slice(modes + LANES, modes + 2 * LANES)
    p_left, z_left = jnp.maximum(p - 1, 0), jnp.maximum(z - 1, 0)
    p_right, z_right = jnp.minimum(p + 1, plane - 1), jnp.minimum(z + 1, planes - 1)
    here = p > 0
    left_block = jnp.where(here, feeds_ref[p_left, :, block].astype(F32), totals_ref[z_left, :, block].astype(F32))
    left_edge = jnp.where(here, feeds_ref[p_left, :, edge].astype(F32), totals_ref[z_left, :, edge].astype(F32))
    left = unfolded(left_edge[:4] + left_edge[4:8])
    left = left + jnp.sum(left_block[:, LAST : LAST + 1] * before, axis=0, keepdims=True)
    left = jnp.where((z > 0) | here, left, 0.0)
    here = p < plane - 1
    near, far = feeds_ref[p_right, :, block], totals_ref[z_right, :, block]
    step = jnp.where(here, step_of(near, coarse), step_of(far, coarse, NEXT))
    flag = jnp.where(here, near.astype(F32), far.astype(F32))
    right_edge = jnp.where(here, feeds_ref[p_right, :, edge].astype(F32), totals_ref[z_right, :, edge].astype(F32))
    moved = advance(step, error, jnp.zeros_like(error))
    right = unfolded(right_edge[8:12] + right_edge[12:])
    right = right + jnp.sum(flag[:, FIRST : FIRST + 1] * moved, axis=0, keepdims=True)
    right = jnp.where((z < planes - 1) | here, right, 0.0)

    error_ref[...] = error
    for j, n in enumerate(around(index_ref, nodes)):
        wide_ref[at(8 + n), :] = around_ref[j : j + 1]
    wide_ref[7:8] = left
    wide_ref[8 + nodes : 9 + nodes] = right
    for c in range(coarse):
        row = pl.ds(8 + index_ref[c], 1)
        wide_ref[row, :] = wide_ref[row, :] + error[c : c + 1]
    found = affected(index_ref, nodes)
    rows_ref[...] = jnp.zeros_like(rows_ref)
    for j, n in enumerate(found):
        rows_ref[j : j + 1] = (
            2.0 * wide_ref[at(8 + n), :] - wide_ref[at(7 + n), :] - wide_ref[at(9 + n), :]
        )
    sent_ref[...] = rows_ref[...].astype(BF16)


def correct(z, p, index, feeds, totals, inside, carry, near, nodes):
    modes = near.shape[1]
    coarse = index.shape[0]
    rows = padded(3 * coarse + 2)
    return pl.pallas_call(
        correct_kernel,
        in_specs=[SMEM] * 3 + [VMEM] * 5,
        out_specs=[VMEM] * 3,
        out_shape=[
            shape((rows, modes), BF16),
            shape((coarse, modes)),
            shape((2 * coarse, totals.shape[0] * coarse), BF16),
        ],
        scratch_shapes=[pltpu.VMEM((nodes + 16, modes), F32), pltpu.VMEM((rows, modes), F32)],
        compiler_params=params(52000),
        name="correct",
    )(z, p, index, feeds, totals, inside, carry, near)


def redo_kernel(me_ref, pattern_ref, a_ref, b_ref, c_ref, d_ref, g_ref, coef_ref, right_ref, inverse_ref, message_ref, res_ref, blocks_ref, rows_ref, sems):
    made = copies(into_blocks([a_ref, b_ref, c_ref, d_ref], blocks_ref), sems)
    coefs = columns_of(coef_ref[...], g_ref.shape[0])
    finished(made)

    @pl.loop(0, g_ref.shape[1])
    def _(c):
        total = operated(blocks_ref, g_ref, pattern_ref, me_ref[0], 0, coefs, c)
        res_ref[:, lanes_of(c)] = right_ref[:, lanes_of(c)] - total

    for c in range(inverse_ref.shape[0]):
        rows_ref[c : c + 1] = res_ref[3 * c + 1 : 3 * c + 2]
    feed = feed_of(rows_ref[...], inverse_ref[...]).astype(BF16)
    for p in range(message_ref.shape[0]):
        message_ref[p] = feed


def redo(me, pattern, parts, gblocks, coef_rows, right_rows, inverse, plane):
    rows, modes = right_rows.shape
    coarse = inverse.shape[0]
    return pl.pallas_call(
        redo_kernel,
        in_specs=[SMEM] * 2 + [ANY] * 4 + [VMEM] * 4,
        out_specs=[VMEM] * 2,
        out_shape=[shape((plane, coarse, modes), BF16), shape((rows, modes))],
        scratch_shapes=[
            pltpu.VMEM((4 * modes // LANES, rows, LANES), BF16),
            pltpu.VMEM((coarse, modes), F32),
            pltpu.SemaphoreType.DMA((16,)),
        ],
        compiler_params=params(52000),
        name="redo",
    )(me, pattern, *parts, gblocks, coef_rows, right_rows, inverse)


def last_local_kernel(index_ref, op_ref, right_ref, rows_ref, sub_ref, base_ref, error_ref, base_out_ref, res_out_ref, res_ref, field_ref):
    nodes = op_ref.shape[0]
    res_ref[...] = right_ref[...] - op_ref[...]
    for j, n in enumerate(affected(index_ref, nodes)):
        res_ref[at(n), :] = rows_ref[j : j + 1]
    res = res_ref[...]
    field_ref[...] = base_ref[...] + jnp.dot(sub_ref[...], res.astype(BF16), preferred_element_type=F32)
    for c in range(error_ref.shape[0]):
        field_ref[at(index_ref[c]), :] = field_ref[at(index_ref[c]), :] + error_ref[c : c + 1]
    base_out_ref[...] = jnp.transpose(field_ref[...])
    res_out_ref[...] = jnp.transpose(res)


def last_local(index, op, right, rows, sub_t, base, error):
    nodes, modes = op.shape
    column = lambda height: pl.BlockSpec((height, LANES), lambda j: (0, j))
    row = pl.BlockSpec((LANES, nodes), lambda j: (j, 0))
    return pl.pallas_call(
        last_local_kernel,
        grid=(modes // LANES,),
        in_specs=[
            SMEM,
            column(nodes),
            column(nodes),
            column(rows.shape[0]),
            pl.BlockSpec((nodes, nodes), lambda j: (0, 0)),
            column(nodes),
            column(error.shape[0]),
        ],
        out_specs=[row, row],
        out_shape=[shape((modes, nodes)), shape((modes, nodes))],
        scratch_shapes=[pltpu.VMEM((nodes, LANES), F32), pltpu.VMEM((nodes, LANES), F32)],
        name="last_local",
    )(index, op, right, rows, sub_t, base, error)


def last_kernel(index_ref, totals_ref, inside_ref, weights_ref, base_ref, out_ref, base_vmem, out_vmem, sems):
    modes, nodes = base_ref.shape
    load = pltpu.make_async_copy(base_ref, base_vmem, sems.at[0])
    load.start()
    planes, coarse, _ = totals_ref.shape
    totals = totals_ref[...].reshape(planes * coarse, modes)
    sums = jnp.dot(weights_ref[...], totals, preferred_element_type=F32)
    error = inside_ref[...] + sums[:coarse] + sums[coarse:]
    high = error.astype(BF16).astype(F32)
    rest = error - high
    mid = rest.astype(BF16).astype(F32)
    terms = jnp.transpose(jnp.concatenate([high, mid, rest - mid], axis=0)).astype(BF16)
    node = lax.broadcasted_iota(jnp.int32, (coarse, nodes), 1)
    row = lax.broadcasted_iota(jnp.int32, (coarse, nodes), 0)
    wanted = jnp.zeros((coarse, nodes), jnp.int32)
    for c in range(coarse):
        wanted = jnp.where(row == c, index_ref[c], wanted)
    onehot = (node == wanted).astype(F32)
    onehot = jnp.concatenate([onehot] * 3, axis=0).astype(BF16)
    load.wait()
    made = []
    for n in range(modes // LANES):
        rows = slice(n * LANES, (n + 1) * LANES)
        out_vmem[rows] = base_vmem[rows] + jnp.dot(terms[rows], onehot, preferred_element_type=F32)
        made.append(pltpu.make_async_copy(out_vmem.at[rows], out_ref.at[rows], sems.at[1 + n]))
        made[-1].start()
    finished(made)


def last(index, totals, inside, weights, base):
    modes, _ = base.shape
    return pl.pallas_call(
        last_kernel,
        in_specs=[SMEM] + [VMEM] * 3 + [ANY],
        out_specs=ANY,
        out_shape=shape(base.shape),
        scratch_shapes=[
            pltpu.VMEM(base.shape, F32),
            pltpu.VMEM(base.shape, F32),
            pltpu.SemaphoreType.DMA((1 + modes // LANES,)),
        ],
        compiler_params=params(52000),
        name="last",
    )(index, totals, inside, weights, base)


def from_neighbours(last_rows, first_rows):
    size = lax.axis_size(SUB)
    up = [(i, i + 1) for i in range(size - 1)]
    left = lax.ppermute(last_rows, SUB, up)
    right = lax.ppermute(first_rows, SUB, [(j, i) for i, j in up])
    return left, right


def over_modes(own):
    swap = [(0, 1), (1, 0)]
    across = lax.ppermute(own, "yl", swap)
    beside = lax.ppermute(own, "core", swap)
    onward = lax.ppermute(across, "core", swap)
    return own, beside, across, onward


def over_modes_directly(own):
    across = lax.ppermute(own, "yl", [(0, 1), (1, 0)])
    diagonal = lax.ppermute(own, MODE, [(0, 3), (1, 2), (2, 1), (3, 0)])
    beside = lax.ppermute(own, "core", [(0, 1), (1, 0)])
    return own, beside, across, diagonal


def shards(right_side, start_field, coefficient, gblocks, pattern, sub_inverse, coarse_index, coarse_inv, coupling):
    me = lax.axis_index(MODE).reshape(1)
    z, p = lax.axis_index("z").reshape(1), lax.axis_index(PLANE).reshape(1)
    planes, plane = lax.axis_size("z"), lax.axis_size(PLANE)
    nodes = start_field.shape[1]
    pattern = jnp.swapaxes(pattern, 1, 2)
    diffs, top, low, last_rows, first_rows = start(start_field)
    parts = over_modes(diffs)
    left, right = from_neighbours(last_rows, first_rows)
    edge_rows = edges(top, low, left, right)
    edge_parts = over_modes_directly(edge_rows)
    rhs, sub_t, field, coef, right_rows, coef_rows = prepare(
        coarse_index, right_side, sub_inverse, start_field, coefficient
    )
    message, base, diffs, near = first_update(
        me, pattern, coarse_index, parts, edge_parts, gblocks, coef, rhs, sub_t, field, coarse_inv, coupling, plane
    )
    parts = over_modes(diffs)
    feeds = lax.all_to_all(message, PLANE, 0, 0, tiled=True)
    totals, inside, weights, carry = plane_totals(p, feeds, planes)
    totals = lax.all_to_all(totals, "z", 0, 0, tiled=True)
    rows, error, plane_weights = correct(z, p, coarse_index, feeds, totals, inside, carry, near, nodes)
    rows = over_modes_directly(rows)
    op = bulk(me, pattern, parts, gblocks, coef)
    held = hold(gblocks, error, gblocks.shape[1])
    message, res_rows = redo(me, pattern, rows, held, coef_rows, right_rows, coarse_inv, plane)
    later = lax.all_to_all(message, PLANE, 0, 0, tiled=True)
    base, residual = last_local(coarse_index, op, rhs, res_rows, sub_t, base, error)
    later_totals, inside = second_plane_totals(later, weights, planes)
    later_totals = lax.all_to_all(later_totals, "z", 0, 0, tiled=True)
    field = last(coarse_index, later_totals, inside, plane_weights, base)
    return field, residual


def solution(mesh):
    split = Mesh(mesh.devices.reshape(8, 4, 2, 2, 2), SUB + MODE)
    placed = (
        P(MODE, SUB),
        P(MODE, SUB),
        P(None, SUB),
        P(None, MODE, None, None, None),
        P(),
        P(SUB, None),
        P(SUB),
        P(SUB, None),
        P(SUB, None),
    )
    return jax.shard_map(shards, mesh=split, in_specs=placed, out_specs=(P(MODE, SUB), P(MODE, SUB)), check_vma=False)
```

```python
import jax
import jax.numpy as jnp
from jax import lax
from jax.experimental import pallas as pl
from jax.experimental.pallas import tpu as pltpu
from jax.sharding import Mesh
from jax.sharding import PartitionSpec as P

SUB = ("z", "x", "yh")
PLANE = ("x", "yh")
MODE = ("yl", "core")
EDGE = 16
LANES = 128
F32 = jnp.float32
BF16 = jnp.bfloat16
VMEM = pl.BlockSpec(memory_space=pltpu.VMEM)
SMEM = pl.BlockSpec(memory_space=pltpu.SMEM)


def params(kib=63600):
    return pltpu.CompilerParams(vmem_limit_bytes=kib * 1024)


def shape(dims, dtype=F32):
    return jax.ShapeDtypeStruct(dims, dtype)


def start_kernel(field_ref, middle_ref, top_ref, low_ref, last_ref, first_ref, rows_ref, sems):
    modes, nodes = field_ref.shape
    made = [
        pltpu.make_async_copy(field_ref.at[pl.ds(j * LANES, LANES)], rows_ref.at[j], sems.at[j])
        for j in range(modes // LANES)
    ]
    for copy in made:
        copy.start()
    for j, copy in enumerate(made):
        copy.wait()
        field = jnp.transpose(rows_ref[j])
        lanes = slice(j * LANES, (j + 1) * LANES)
        diffs = 2.0 * field - pltpu.roll(field, 1, 0) - pltpu.roll(field, nodes - 1, 0)
        middle_ref[:, lanes] = diffs[EDGE : nodes - EDGE].astype(BF16)
        top_ref[:, lanes] = field[: EDGE + 8]
        low_ref[:, lanes] = field[nodes - EDGE - 8 :]
        last_ref[:, lanes] = jnp.broadcast_to(field[nodes - 1 :], (8, LANES))
        first_ref[:, lanes] = jnp.broadcast_to(field[:1], (8, LANES))


def start(field):
    modes, nodes = field.shape
    return pl.pallas_call(
        start_kernel,
        in_specs=[pl.BlockSpec(memory_space=pltpu.HBM)],
        out_specs=[VMEM] * 5,
        out_shape=[
            shape((nodes - 2 * EDGE, modes), BF16),
            shape((EDGE + 8, modes)),
            shape((EDGE + 8, modes)),
            shape((8, modes)),
            shape((8, modes)),
        ],
        scratch_shapes=[
            pltpu.VMEM((modes // LANES, LANES, nodes), F32),
            pltpu.SemaphoreType.DMA((modes // LANES,)),
        ],
        compiler_params=params(63600),
        name="start",
    )(field)


def affected(index_ref, nodes):
    found = []
    for c in range(index_ref.shape[0]):
        for off in (-1, 0, 1):
            found.append(jnp.clip(index_ref[c] + off, 0, nodes - 1))
    return found + [0, nodes - 1]


def around(index_ref, nodes):
    found = []
    for c in range(index_ref.shape[0]):
        for off in (-2, -1, 0, 1, 2):
            found.append(jnp.clip(index_ref[c] + off, 0, nodes - 1))
    return found + [0, 1, nodes - 2, nodes - 1]


def padded(count):
    return -(-count // 16) * 16


def at(row):
    return slice(row, row + 1) if isinstance(row, int) else pl.ds(row, 1)


def prepare_kernel(index_ref, right_ref, inverse_ref, field_ref, coef_ref, right_t_ref, inverse_t_ref, field_t_ref, coef_t_ref, right_rows_ref, coef_rows_ref):
    right_t_ref[...] = jnp.transpose(right_ref[...])
    inverse_t_ref[...] = jnp.transpose(inverse_ref[...].astype(F32)).astype(BF16)
    field_t_ref[...] = jnp.transpose(field_ref[...])
    terms, nodes = coef_ref.shape
    found = affected(index_ref, nodes)
    right_rows_ref[...] = jnp.zeros_like(right_rows_ref)
    for j, n in enumerate(found):
        right_rows_ref[j : j + 1] = right_t_ref[at(n), :]

    @pl.when(pl.program_id(0) == 0)
    def _():
        wide = jnp.concatenate([coef_ref[...], jnp.zeros((LANES - terms, nodes), F32)], axis=0)
        coef_t_ref[...] = jnp.transpose(wide)
        coef_rows_ref[...] = jnp.zeros_like(coef_rows_ref)
        for j, n in enumerate(found):
            coef_rows_ref[j : j + 1] = coef_t_ref[at(n), :]


def prepare(index, right_side, sub_inverse, field, coefficient):
    modes, nodes = right_side.shape
    count = padded(3 * index.shape[0] + 2)
    rows = lambda width: pl.BlockSpec((LANES, width), lambda j: (j, 0))
    column = lambda height: pl.BlockSpec((height, LANES), lambda j: (0, j))
    fixed = lambda height: pl.BlockSpec((height, LANES), lambda j: (0, 0))
    return pl.pallas_call(
        prepare_kernel,
        grid=(modes // LANES,),
        in_specs=[
            SMEM,
            rows(nodes),
            rows(nodes),
            rows(nodes),
            pl.BlockSpec(coefficient.shape, lambda j: (0, 0)),
        ],
        out_specs=[column(nodes)] * 3 + [fixed(nodes), column(count), fixed(count)],
        out_shape=[
            shape((nodes, modes)),
            shape((nodes, nodes), BF16),
            shape((nodes, modes)),
            shape((nodes, LANES)),
            shape((count, modes)),
            shape((count, LANES)),
        ],
        name="prepare",
    )(index, right_side, sub_inverse, field, coefficient)


def edge_kernel(top_ref, low_ref, left_ref, right_ref, edge_ref):
    top = top_ref[...]
    before = jnp.concatenate([left_ref[:1], top[: EDGE - 1]], axis=0)
    edge_ref[:EDGE] = (2.0 * top[:EDGE] - before - top[1 : EDGE + 1]).astype(BF16)
    low = low_ref[...]
    after = jnp.concatenate([low[9:], right_ref[:1]], axis=0)
    edge_ref[EDGE:] = (2.0 * low[8:] - low[7:-1] - after).astype(BF16)


def edges(top, low, left, right):
    return pl.pallas_call(
        edge_kernel,
        in_specs=[VMEM] * 4,
        out_specs=VMEM,
        out_shape=shape((2 * EDGE, top.shape[1]), BF16),
        compiler_params=params(16384),
        name="edges",
    )(top, low, left, right)


HBM = pl.BlockSpec(memory_space=pltpu.HBM)
ANY = pl.BlockSpec(memory_space=pl.ANY)


def copies(pairs, sems):
    made = [pltpu.make_async_copy(a, b, sems.at[n]) for n, (a, b) in enumerate(pairs)]
    for copy in made:
        copy.start()
    return made


def finished(made):
    for copy in made:
        copy.wait()


def into_blocks(part_refs, blocks_ref, rows=slice(None)):
    each = part_refs[0].shape[-1] // LANES
    return [
        (part.at[:, pl.ds(b * LANES, LANES)], blocks_ref.at[n * each + b, rows])
        for n, part in enumerate(part_refs)
        for b in range(each)
    ]


def operated(blocks_ref, g_ref, pattern_ref, me, first, coefs, c):
    total = None
    own = pattern_ref.shape[2] // 4
    for k in range(g_ref.shape[0]):
        rows = []
        for t in range(g_ref.shape[2]):
            row = pattern_ref[k, t, me * own + first + c]
            owner = lax.div(row, own)
            row = (owner ^ me) * own + lax.rem(row, own)
            rows.append(blocks_ref[row])
        weights = g_ref[k, c].reshape(-1, LANES)
        product = jnp.dot(jnp.concatenate(rows, axis=1), weights, preferred_element_type=F32)
        scaled = coefs[k] * product
        total = scaled if total is None else total + scaled
    return total


def weights_into(g_ref, g_vmem, sems, first):
    return [
        pltpu.make_async_copy(g_ref.at[:, c], g_vmem.at[:, c], sems.at[first + c])
        for c in range(g_ref.shape[1])
    ]


def wait_weights(g_ref, g_vmem, sems, first, c):
    pltpu.make_async_copy(g_ref.at[:, c], g_vmem.at[:, c], sems.at[first + c]).wait()


def columns_of(coef, count):
    return [coef[:, k : k + 1] for k in range(count)]


def lanes_of(c):
    return pl.ds(pl.multiple_of(c * LANES, LANES), LANES)


def bulk_kernel(me_ref, pattern_ref, a_ref, b_ref, c_ref, d_ref, g_hbm, coef_ref, out_ref, blocks_ref, g_ref, sems):
    weights = weights_into(g_hbm, g_ref, sems, 16)
    weights[0].start()
    made = copies(into_blocks([a_ref, b_ref, c_ref, d_ref], blocks_ref), sems)
    for copy in weights[1:]:
        copy.start()
    coefs = columns_of(coef_ref[...], g_ref.shape[0])
    finished(made)

    @pl.loop(0, g_ref.shape[1])
    def _(c):
        wait_weights(g_hbm, g_ref, sems, 16, c)
        out_ref[:, lanes_of(c)] = operated(blocks_ref, g_ref, pattern_ref, me_ref[0], 0, coefs, c)


def bulk(me, pattern, parts, gblocks, coef):
    rows, modes = parts[0].shape
    return pl.pallas_call(
        bulk_kernel,
        in_specs=[SMEM, SMEM] + [ANY] * 5 + [VMEM],
        out_specs=VMEM,
        out_shape=shape((rows, modes)),
        scratch_shapes=[
            pltpu.VMEM((4 * modes // LANES, rows, LANES), BF16),
            pltpu.VMEM(gblocks.shape, BF16),
            pltpu.SemaphoreType.DMA((16 + gblocks.shape[1],)),
        ],
        compiler_params=params(52000),
        name="whole",
    )(me, pattern, *parts, gblocks, coef)


def hold_kernel(g_ref, after_ref, out_ref, sems):
    del after_ref
    made = [
        pltpu.make_async_copy(g_ref.at[:, c], out_ref.at[:, c], sems.at[c])
        for c in range(out_ref.shape[1])
    ]
    for copy in made:
        copy.start()
    finished(made)


def hold(gblocks, after, count):
    terms, _, *rest = gblocks.shape
    return pl.pallas_call(
        hold_kernel,
        in_specs=[HBM, ANY],
        out_specs=VMEM,
        out_shape=shape((terms, count, *rest), BF16),
        scratch_shapes=[pltpu.SemaphoreType.DMA((count,))],
        compiler_params=params(16384),
    )(gblocks, after)


def two_terms(value):
    high = value.astype(BF16).astype(F32)
    return high, value - high


def feed_of(rows, inverse):
    coarse = inverse.shape[0]
    inverse_t = jnp.transpose(inverse)
    feed = inverse_t[:, :1] * rows[:1]
    for c in range(1, coarse):
        feed = feed + inverse_t[:, c : c + 1] * rows[c : c + 1]
    return feed


def flags(index_ref, node):
    coarse = index_ref.shape[0]
    row = lax.broadcasted_iota(jnp.int32, (coarse, LANES), 0)
    found = jnp.zeros((coarse, LANES), F32)
    for c in range(coarse):
        found = jnp.where((row == c) & (index_ref[c] == node), 1.0, found)
    return found


def folded(row):
    count = row.shape[1] // LANES
    return jnp.concatenate([row[:, b * LANES : (b + 1) * LANES] for b in range(count)], axis=0)


def unfolded(rows):
    return jnp.concatenate([rows[b : b + 1] for b in range(rows.shape[0])], axis=1)


LAST, FIRST, NEXT = 32, 33, 48


def first_kernel(me_ref, pattern_ref, index_ref, a_ref, b_ref, c_ref, d_ref, ea_ref, eb_ref, ec_ref, ed_ref, g_hbm, coef_ref, right_ref, sub_ref, field_ref, inverse_ref, coupling_ref, message_ref, base_ref, diffs_ref, around_ref, blocks_ref, res_ref, sub_vmem, base_vmem, diffs_vmem, rows_ref, g_ref, sems):
    nodes, _ = field_ref.shape
    coarse = inverse_ref.shape[0]
    inner = pl.ds(EDGE, nodes - 2 * EDGE)
    weights = weights_into(g_hbm, g_ref, sems, 51)
    weights[0].start()
    made = copies(
        into_blocks([a_ref, b_ref, c_ref, d_ref], blocks_ref, inner)
        + into_blocks([r.at[pl.ds(0, EDGE)] for r in (ea_ref, eb_ref, ec_ref, ed_ref)], blocks_ref, pl.ds(0, EDGE))
        + into_blocks([r.at[pl.ds(EDGE, EDGE)] for r in (ea_ref, eb_ref, ec_ref, ed_ref)], blocks_ref, pl.ds(nodes - EDGE, EDGE))
        + [(right_ref, res_ref)],
        sems,
    )
    for copy in weights[1:]:
        copy.start()
    later = [
        pltpu.make_async_copy(sub_ref, sub_vmem, sems.at[49]),
        pltpu.make_async_copy(field_ref, base_vmem, sems.at[50]),
    ]
    for copy in later:
        copy.start()
    coefs = columns_of(coef_ref[...], g_ref.shape[0])
    finished(made)

    @pl.loop(0, g_ref.shape[1])
    def _(c):
        wait_weights(g_hbm, g_ref, sems, 51, c)
        total = operated(blocks_ref, g_ref, pattern_ref, me_ref[0], 0, coefs, c)
        res_ref[:, lanes_of(c)] = res_ref[:, lanes_of(c)] - total

    finished(later)
    for c in range(coarse):
        rows_ref[c : c + 1] = res_ref[pl.ds(index_ref[c], 1), :]
    feed = feed_of(rows_ref[...], inverse_ref[...])
    local = jnp.dot(sub_vmem[...], res_ref[...].astype(BF16), preferred_element_type=F32)
    base = base_vmem[...] + local
    base_vmem[...] = base
    out = [pltpu.make_async_copy(base_vmem, base_ref, sems.at[0])]
    out[0].start()
    diffs = 2.0 * base - pltpu.roll(base, 1, 0) - pltpu.roll(base, nodes - 1, 0)
    diffs_vmem[...] = diffs.astype(BF16)
    out.append(pltpu.make_async_copy(diffs_vmem, diffs_ref, sems.at[1]))
    out[1].start()

    lane = lax.broadcasted_iota(jnp.int32, (coarse, LANES), 1)
    high, low = two_terms(
        jnp.concatenate([jnp.transpose(coupling_ref[...]), jnp.zeros((coarse, LANES - coarse), F32)], axis=1)
    )
    at_last, at_first = flags(index_ref, nodes - 1), flags(index_ref, 0)
    block = high + pltpu.roll(low, coarse, 1)
    block = block + jnp.where(lane == LAST, at_last, 0.0) + jnp.where(lane == FIRST, at_first, 0.0)
    first = base[:1] + jnp.sum(at_first[:, :1] * feed.astype(BF16).astype(F32), axis=0, keepdims=True)
    edge = jnp.concatenate(
        two_terms(folded(base[nodes - 1 :])) + two_terms(folded(first)), axis=0
    )
    sent = jnp.concatenate([feed, block, edge], axis=1).astype(BF16)
    for p in range(message_ref.shape[0]):
        message_ref[p] = sent
    for j, n in enumerate(around(index_ref, nodes)):
        around_ref[j : j + 1] = base_vmem[at(n), :]
    finished(out)


def first_update(me, pattern, index, parts, edge_parts, gblocks, coef, right, sub_t, field, inverse, coupling, plane):
    nodes, modes = right.shape
    coarse = inverse.shape[0]
    return pl.pallas_call(
        first_kernel,
        in_specs=[SMEM] * 3 + [ANY] * 9 + [VMEM] + [ANY] * 3 + [VMEM] * 2,
        out_specs=[VMEM, ANY, ANY, VMEM],
        out_shape=[
            shape((plane, coarse, modes + 2 * LANES), BF16),
            shape((nodes, modes)),
            shape((nodes, modes), BF16),
            shape((padded(5 * coarse + 4), modes)),
        ],
        scratch_shapes=[
            pltpu.VMEM((4 * modes // LANES, nodes, LANES), BF16),
            pltpu.VMEM((nodes, modes), F32),
            pltpu.VMEM((nodes, nodes), BF16),
            pltpu.VMEM((nodes, modes), F32),
            pltpu.VMEM((nodes, modes), BF16),
            pltpu.VMEM((coarse, modes), F32),
            pltpu.VMEM(gblocks.shape, BF16),
            pltpu.SemaphoreType.DMA((51 + gblocks.shape[1],)),
        ],
        compiler_params=params(52000),
        name="first_update",
    )(me, pattern, index, *parts, *edge_parts, gblocks, coef, right, sub_t, field, inverse, coupling)


def advance(coupling_t, state, push):
    moved = push
    for c in range(state.shape[0]):
        moved = moved + coupling_t[:, c : c + 1] * state[c : c + 1]
    return moved


def step_of(block, coarse, at=0):
    block = block.astype(F32)
    if at:
        block = pltpu.roll(block, LANES - at, 1)
    return block + pltpu.roll(block, LANES - coarse, 1)


def lanes_and_rows(coarse):
    row = lax.broadcasted_iota(jnp.int32, (coarse, LANES), 0)
    lane = lax.broadcasted_iota(jnp.int32, (coarse, LANES), 1)
    return row, lane


def side_by_side(squares):
    coarse = squares[0].shape[0]
    _, lane = lanes_and_rows(coarse)
    total = None
    for n, square in enumerate(squares):
        square = jnp.where(lane < coarse, square, 0.0)
        square = pltpu.roll(square, n * coarse, 1) if n else square
        total = square if total is None else total + square
    return total


def terms_of(weights):
    return jnp.concatenate(two_terms(weights), axis=0).astype(BF16)


def plane_kernel(feeds_ref, out_ref, weights_ref):
    plane, coarse, width = feeds_ref.shape
    modes = width - 2 * LANES
    row, lane = lanes_and_rows(coarse)
    one = (row == lane).astype(F32)
    whole, wholes = one, []
    for q in range(plane - 1, -1, -1):
        wholes.append(whole)
        whole = advance(whole, step_of(feeds_ref[q, :, modes : modes + LANES], coarse), jnp.zeros_like(one))
    totals = terms_of(side_by_side(wholes[::-1]))
    weights_ref[...] = totals
    feeds = feeds_ref[:, :, :modes].reshape(plane * coarse, modes)
    sums = jnp.dot(totals, feeds, preferred_element_type=F32)
    state = sums[:coarse] + sums[coarse:]
    matrix = jnp.where(lane < coarse, whole, 0.0)
    high, low = two_terms(matrix)
    first = feeds_ref[0, :, modes : modes + LANES].astype(F32)
    final = feeds_ref[plane - 1, :, modes : modes + LANES].astype(F32)
    block = high + pltpu.roll(low, coarse, 1)
    block = block + jnp.where(lane == LAST, final, 0.0) + jnp.where(lane == FIRST, first, 0.0)
    block = block + jnp.where((lane >= NEXT) & (lane < NEXT + 2 * coarse), pltpu.roll(first, NEXT, 1), 0.0)
    edge = jnp.where(
        row < coarse // 2,
        feeds_ref[plane - 1, :, modes + LANES :].astype(F32),
        feeds_ref[0, :, modes + LANES :].astype(F32),
    )
    sent = jnp.concatenate([state, block, edge], axis=1).astype(BF16)
    for z in range(out_ref.shape[0]):
        out_ref[z] = sent


def plane_totals(feeds, planes):
    plane, coarse, width = feeds.shape
    return pl.pallas_call(
        plane_kernel,
        in_specs=[VMEM],
        out_specs=[VMEM] * 2,
        out_shape=[
            shape((planes, coarse, width), BF16),
            shape((2 * coarse, plane * coarse), BF16),
        ],
        compiler_params=params(52000),
        name="plane_totals",
    )(feeds)


def inside_kernel(p_ref, feeds_ref, totals_ref, inside_ref, weights_ref, carry_ref):
    plane, coarse, width = feeds_ref.shape
    modes = width - 2 * LANES
    p = p_ref[0]
    row, lane = lanes_and_rows(coarse)
    one = (row == lane).astype(F32)
    before, befores = jnp.zeros_like(one), []
    for q in range(plane - 1, -1, -1):
        before = jnp.where(q == p - 1, one, before)
        befores.append(before)
        before = advance(before, step_of(feeds_ref[q, :, modes : modes + LANES], coarse), jnp.zeros_like(one))
    carry_ref[...] = jnp.where(p == 0, one, before)
    excluding = side_by_side(befores[::-1])
    own = step_of(feeds_ref[p, :, modes : modes + LANES], coarse)
    including = advance(own, excluding, (lane == p * coarse + row).astype(F32))
    weights_ref[...] = jnp.concatenate([totals_ref[...], terms_of(including)], axis=0)
    feeds = feeds_ref[:, :, :modes].reshape(plane * coarse, modes)
    sums = jnp.dot(terms_of(excluding), feeds, preferred_element_type=F32)
    inside_ref[...] = sums[:coarse] + sums[coarse:]


def inside_plane(p, feeds, totals):
    plane, coarse, width = feeds.shape
    return pl.pallas_call(
        inside_kernel,
        in_specs=[SMEM, VMEM, VMEM],
        out_specs=[VMEM] * 3,
        out_shape=[
            shape((coarse, width - 2 * LANES)),
            shape((4 * coarse, plane * coarse), BF16),
            shape((coarse, LANES)),
        ],
        compiler_params=params(52000),
        name="inside_plane",
    )(p, feeds, totals)


def second_plane_kernel(feeds_ref, weights_ref, out_ref, inside_ref):
    plane, coarse, modes = feeds_ref.shape
    feeds = feeds_ref[...].reshape(plane * coarse, modes)
    sums = jnp.dot(weights_ref[...], feeds, preferred_element_type=F32)
    state = (sums[:coarse] + sums[coarse : 2 * coarse]).astype(BF16)
    inside_ref[...] = sums[2 * coarse : 3 * coarse] + sums[3 * coarse :]
    for z in range(out_ref.shape[0]):
        out_ref[z] = state


def second_plane_totals(feeds, weights, planes):
    _, coarse, modes = feeds.shape
    return pl.pallas_call(
        second_plane_kernel,
        in_specs=[VMEM] * 2,
        out_specs=[VMEM] * 2,
        out_shape=[shape((planes, coarse, modes), BF16), shape((coarse, modes))],
        compiler_params=params(52000),
        name="second_plane_totals",
    )(feeds, weights)


def correct_kernel(z_ref, p_ref, index_ref, feeds_ref, totals_ref, inside_ref, carry_ref, around_ref, sent_ref, error_ref, weights_ref, wide_ref, rows_ref):
    nodes, modes = wide_ref.shape[0] - 16, wide_ref.shape[1]
    plane, planes = feeds_ref.shape[0], totals_ref.shape[0]
    z, p = z_ref[0], p_ref[0]
    coarse = index_ref.shape[0]
    none = jnp.zeros((coarse, LANES), F32)
    factor = none
    factors = []
    for q in range(planes - 1, -1, -1):
        factor = jnp.where(q == z - 1, carry_ref[...], factor)
        factors.append(factor)
        factor = advance(factor, step_of(totals_ref[q, :, modes : modes + LANES], coarse), none)
    weights = side_by_side(factors[::-1])
    totals = totals_ref[:, :, :modes].reshape(planes * coarse, modes)
    sums = jnp.dot(terms_of(weights), totals, preferred_element_type=F32)
    before = inside_ref[...] + sums[:coarse] + sums[coarse:]
    own = step_of(feeds_ref[p, :, modes : modes + LANES], coarse)
    error = advance(own, before, feeds_ref[p, :, :modes].astype(F32))
    weights_ref[...] = terms_of(advance(own, weights, none))

    block, edge = slice(modes, modes + LANES), slice(modes + LANES, modes + 2 * LANES)
    p_left, z_left = jnp.maximum(p - 1, 0), jnp.maximum(z - 1, 0)
    p_right, z_right = jnp.minimum(p + 1, plane - 1), jnp.minimum(z + 1, planes - 1)
    here = p > 0
    left_block = jnp.where(here, feeds_ref[p_left, :, block].astype(F32), totals_ref[z_left, :, block].astype(F32))
    left_edge = jnp.where(here, feeds_ref[p_left, :, edge].astype(F32), totals_ref[z_left, :, edge].astype(F32))
    left = unfolded(left_edge[:4] + left_edge[4:8])
    left = left + jnp.sum(left_block[:, LAST : LAST + 1] * before, axis=0, keepdims=True)
    left = jnp.where((z > 0) | here, left, 0.0)
    here = p < plane - 1
    near, far = feeds_ref[p_right, :, block], totals_ref[z_right, :, block]
    step = jnp.where(here, step_of(near, coarse), step_of(far, coarse, NEXT))
    flag = jnp.where(here, near.astype(F32), far.astype(F32))
    right_edge = jnp.where(here, feeds_ref[p_right, :, edge].astype(F32), totals_ref[z_right, :, edge].astype(F32))
    moved = advance(step, error, jnp.zeros_like(error))
    right = unfolded(right_edge[8:12] + right_edge[12:])
    right = right + jnp.sum(flag[:, FIRST : FIRST + 1] * moved, axis=0, keepdims=True)
    right = jnp.where((z < planes - 1) | here, right, 0.0)

    error_ref[...] = error
    for j, n in enumerate(around(index_ref, nodes)):
        wide_ref[at(8 + n), :] = around_ref[j : j + 1]
    wide_ref[7:8] = left
    wide_ref[8 + nodes : 9 + nodes] = right
    for c in range(coarse):
        row = pl.ds(8 + index_ref[c], 1)
        wide_ref[row, :] = wide_ref[row, :] + error[c : c + 1]
    found = affected(index_ref, nodes)
    rows_ref[...] = jnp.zeros_like(rows_ref)
    for j, n in enumerate(found):
        rows_ref[j : j + 1] = (
            2.0 * wide_ref[at(8 + n), :] - wide_ref[at(7 + n), :] - wide_ref[at(9 + n), :]
        )
    sent_ref[...] = rows_ref[...].astype(BF16)


def correct(z, p, index, feeds, totals, inside, carry, near, nodes):
    modes = near.shape[1]
    coarse = index.shape[0]
    rows = padded(3 * coarse + 2)
    return pl.pallas_call(
        correct_kernel,
        in_specs=[SMEM] * 3 + [VMEM] * 5,
        out_specs=[VMEM] * 3,
        out_shape=[
            shape((rows, modes), BF16),
            shape((coarse, modes)),
            shape((2 * coarse, totals.shape[0] * coarse), BF16),
        ],
        scratch_shapes=[pltpu.VMEM((nodes + 16, modes), F32), pltpu.VMEM((rows, modes), F32)],
        compiler_params=params(52000),
        name="correct",
    )(z, p, index, feeds, totals, inside, carry, near)


def redo_kernel(me_ref, pattern_ref, a_ref, b_ref, c_ref, d_ref, g_ref, coef_ref, right_ref, inverse_ref, message_ref, res_ref, blocks_ref, rows_ref, sems):
    made = copies(into_blocks([a_ref, b_ref, c_ref, d_ref], blocks_ref), sems)
    coefs = columns_of(coef_ref[...], g_ref.shape[0])
    finished(made)

    @pl.loop(0, g_ref.shape[1])
    def _(c):
        total = operated(blocks_ref, g_ref, pattern_ref, me_ref[0], 0, coefs, c)
        res_ref[:, lanes_of(c)] = right_ref[:, lanes_of(c)] - total

    for c in range(inverse_ref.shape[0]):
        rows_ref[c : c + 1] = res_ref[3 * c + 1 : 3 * c + 2]
    feed = feed_of(rows_ref[...], inverse_ref[...]).astype(BF16)
    for p in range(message_ref.shape[0]):
        message_ref[p] = feed


def redo(me, pattern, parts, gblocks, coef_rows, right_rows, inverse, plane):
    rows, modes = right_rows.shape
    coarse = inverse.shape[0]
    return pl.pallas_call(
        redo_kernel,
        in_specs=[SMEM] * 2 + [ANY] * 4 + [VMEM] * 4,
        out_specs=[VMEM] * 2,
        out_shape=[shape((plane, coarse, modes), BF16), shape((rows, modes))],
        scratch_shapes=[
            pltpu.VMEM((4 * modes // LANES, rows, LANES), BF16),
            pltpu.VMEM((coarse, modes), F32),
            pltpu.SemaphoreType.DMA((16,)),
        ],
        compiler_params=params(52000),
        name="redo",
    )(me, pattern, *parts, gblocks, coef_rows, right_rows, inverse)


def last_local_kernel(index_ref, op_ref, right_ref, rows_ref, sub_ref, base_ref, error_ref, base_out_ref, res_out_ref, res_ref, field_ref):
    nodes = op_ref.shape[0]
    res_ref[...] = right_ref[...] - op_ref[...]
    for j, n in enumerate(affected(index_ref, nodes)):
        res_ref[at(n), :] = rows_ref[j : j + 1]
    res = res_ref[...]
    field_ref[...] = base_ref[...] + jnp.dot(sub_ref[...], res.astype(BF16), preferred_element_type=F32)
    for c in range(error_ref.shape[0]):
        field_ref[at(index_ref[c]), :] = field_ref[at(index_ref[c]), :] + error_ref[c : c + 1]
    base_out_ref[...] = jnp.transpose(field_ref[...])
    res_out_ref[...] = jnp.transpose(res)


def last_local(index, op, right, rows, sub_t, base, error):
    nodes, modes = op.shape
    column = lambda height: pl.BlockSpec((height, LANES), lambda j: (0, j))
    row = pl.BlockSpec((LANES, nodes), lambda j: (j, 0))
    return pl.pallas_call(
        last_local_kernel,
        grid=(modes // LANES,),
        in_specs=[
            SMEM,
            column(nodes),
            column(nodes),
            column(rows.shape[0]),
            pl.BlockSpec((nodes, nodes), lambda j: (0, 0)),
            column(nodes),
            column(error.shape[0]),
        ],
        out_specs=[row, row],
        out_shape=[shape((modes, nodes)), shape((modes, nodes))],
        scratch_shapes=[pltpu.VMEM((nodes, LANES), F32), pltpu.VMEM((nodes, LANES), F32)],
        name="last_local",
    )(index, op, right, rows, sub_t, base, error)


def last_kernel(index_ref, totals_ref, inside_ref, weights_ref, base_ref, out_ref, base_vmem, out_vmem, sems):
    modes, nodes = base_ref.shape
    load = pltpu.make_async_copy(base_ref, base_vmem, sems.at[0])
    load.start()
    planes, coarse, _ = totals_ref.shape
    totals = totals_ref[...].reshape(planes * coarse, modes)
    sums = jnp.dot(weights_ref[...], totals, preferred_element_type=F32)
    error = inside_ref[...] + sums[:coarse] + sums[coarse:]
    high = error.astype(BF16).astype(F32)
    rest = error - high
    mid = rest.astype(BF16).astype(F32)
    terms = jnp.transpose(jnp.concatenate([high, mid, rest - mid], axis=0)).astype(BF16)
    node = lax.broadcasted_iota(jnp.int32, (coarse, nodes), 1)
    row = lax.broadcasted_iota(jnp.int32, (coarse, nodes), 0)
    wanted = jnp.zeros((coarse, nodes), jnp.int32)
    for c in range(coarse):
        wanted = jnp.where(row == c, index_ref[c], wanted)
    onehot = (node == wanted).astype(F32)
    onehot = jnp.concatenate([onehot] * 3, axis=0).astype(BF16)
    load.wait()
    made = []
    for n in range(modes // LANES):
        rows = slice(n * LANES, (n + 1) * LANES)
        out_vmem[rows] = base_vmem[rows] + jnp.dot(terms[rows], onehot, preferred_element_type=F32)
        made.append(pltpu.make_async_copy(out_vmem.at[rows], out_ref.at[rows], sems.at[1 + n]))
        made[-1].start()
    finished(made)


def last(index, totals, inside, weights, base):
    modes, _ = base.shape
    return pl.pallas_call(
        last_kernel,
        in_specs=[SMEM] + [VMEM] * 3 + [ANY],
        out_specs=ANY,
        out_shape=shape(base.shape),
        scratch_shapes=[
            pltpu.VMEM(base.shape, F32),
            pltpu.VMEM(base.shape, F32),
            pltpu.SemaphoreType.DMA((1 + modes // LANES,)),
        ],
        compiler_params=params(52000),
        name="last",
    )(index, totals, inside, weights, base)


def from_neighbours(last_rows, first_rows):
    size = lax.axis_size(SUB)
    up = [(i, i + 1) for i in range(size - 1)]
    left = lax.ppermute(last_rows, SUB, up)
    right = lax.ppermute(first_rows, SUB, [(j, i) for i, j in up])
    return left, right


def over_modes(own):
    swap = [(0, 1), (1, 0)]
    across = lax.ppermute(own, "yl", swap)
    beside = lax.ppermute(own, "core", swap)
    onward = lax.ppermute(across, "core", swap)
    return own, beside, across, onward


def over_modes_directly(own):
    across = lax.ppermute(own, "yl", [(0, 1), (1, 0)])
    diagonal = lax.ppermute(own, MODE, [(0, 3), (1, 2), (2, 1), (3, 0)])
    beside = lax.ppermute(own, "core", [(0, 1), (1, 0)])
    return own, beside, across, diagonal


def shards(right_side, start_field, coefficient, gblocks, pattern, sub_inverse, coarse_index, coarse_inv, coupling):
    me = lax.axis_index(MODE).reshape(1)
    z, p = lax.axis_index("z").reshape(1), lax.axis_index(PLANE).reshape(1)
    planes, plane = lax.axis_size("z"), lax.axis_size(PLANE)
    nodes = start_field.shape[1]
    pattern = jnp.swapaxes(pattern, 1, 2)
    diffs, top, low, last_rows, first_rows = start(start_field)
    parts = over_modes(diffs)
    left, right = from_neighbours(last_rows, first_rows)
    edge_rows = edges(top, low, left, right)
    edge_parts = over_modes_directly(edge_rows)
    rhs, sub_t, field, coef, right_rows, coef_rows = prepare(
        coarse_index, right_side, sub_inverse, start_field, coefficient
    )
    message, base, diffs, near = first_update(
        me, pattern, coarse_index, parts, edge_parts, gblocks, coef, rhs, sub_t, field, coarse_inv, coupling, plane
    )
    parts = over_modes(diffs)
    feeds = lax.all_to_all(message, PLANE, 0, 0, tiled=True)
    totals, weights = plane_totals(feeds, planes)
    inside, weights, carry = inside_plane(p, feeds, weights)
    totals = lax.all_to_all(totals, "z", 0, 0, tiled=True)
    rows, error, plane_weights = correct(z, p, coarse_index, feeds, totals, inside, carry, near, nodes)
    rows = over_modes_directly(rows)
    op = bulk(me, pattern, parts, gblocks, coef)
    held = hold(gblocks, error, gblocks.shape[1])
    message, res_rows = redo(me, pattern, rows, held, coef_rows, right_rows, coarse_inv, plane)
    later = lax.all_to_all(message, PLANE, 0, 0, tiled=True)
    base, residual = last_local(coarse_index, op, rhs, res_rows, sub_t, base, error)
    later_totals, inside = second_plane_totals(later, weights, planes)
    later_totals = lax.all_to_all(later_totals, "z", 0, 0, tiled=True)
    field = last(coarse_index, later_totals, inside, plane_weights, base)
    return field, residual


def solution(mesh):
    split = Mesh(mesh.devices.reshape(8, 4, 2, 2, 2), SUB + MODE)
    placed = (
        P(MODE, SUB),
        P(MODE, SUB),
        P(None, SUB),
        P(None, MODE, None, None, None),
        P(),
        P(SUB, None),
        P(SUB),
        P(SUB, None),
        P(SUB, None),
    )
    return jax.shard_map(shards, mesh=split, in_specs=placed, out_specs=(P(MODE, SUB), P(MODE, SUB)), check_vma=False)
```

```python
import jax
import jax.numpy as jnp
from jax import lax
from jax.experimental import pallas as pl
from jax.experimental.pallas import tpu as pltpu
from jax.sharding import Mesh
from jax.sharding import PartitionSpec as P

SUB = ("z", "x", "yh")
PLANE = ("x", "yh")
MODE = ("yl", "core")
EDGE = 16
LANES = 128
F32 = jnp.float32
BF16 = jnp.bfloat16
VMEM = pl.BlockSpec(memory_space=pltpu.VMEM)
SMEM = pl.BlockSpec(memory_space=pltpu.SMEM)


def params(kib=63600):
    return pltpu.CompilerParams(vmem_limit_bytes=kib * 1024)


def shape(dims, dtype=F32):
    return jax.ShapeDtypeStruct(dims, dtype)


def start_kernel(field_ref, middle_ref, top_ref, low_ref, last_ref, first_ref, rows_ref, sems):
    modes, nodes = field_ref.shape
    made = [
        pltpu.make_async_copy(field_ref.at[pl.ds(j * LANES, LANES)], rows_ref.at[j], sems.at[j])
        for j in range(modes // LANES)
    ]
    for copy in made:
        copy.start()
    for j, copy in enumerate(made):
        copy.wait()
        field = jnp.transpose(rows_ref[j])
        lanes = slice(j * LANES, (j + 1) * LANES)
        diffs = 2.0 * field - pltpu.roll(field, 1, 0) - pltpu.roll(field, nodes - 1, 0)
        middle_ref[:, lanes] = diffs[EDGE : nodes - EDGE].astype(BF16)
        top_ref[:, lanes] = field[: EDGE + 8]
        low_ref[:, lanes] = field[nodes - EDGE - 8 :]
        last_ref[:, lanes] = jnp.broadcast_to(field[nodes - 1 :], (8, LANES))
        first_ref[:, lanes] = jnp.broadcast_to(field[:1], (8, LANES))


def start(field):
    modes, nodes = field.shape
    return pl.pallas_call(
        start_kernel,
        in_specs=[pl.BlockSpec(memory_space=pltpu.HBM)],
        out_specs=[VMEM] * 5,
        out_shape=[
            shape((nodes - 2 * EDGE, modes), BF16),
            shape((EDGE + 8, modes)),
            shape((EDGE + 8, modes)),
            shape((8, modes)),
            shape((8, modes)),
        ],
        scratch_shapes=[
            pltpu.VMEM((modes // LANES, LANES, nodes), F32),
            pltpu.SemaphoreType.DMA((modes // LANES,)),
        ],
        compiler_params=params(63600),
        name="start",
    )(field)


def affected(index_ref, nodes):
    found = []
    for c in range(index_ref.shape[0]):
        for off in (-1, 0, 1):
            found.append(jnp.clip(index_ref[c] + off, 0, nodes - 1))
    return found + [0, nodes - 1]


def around(index_ref, nodes):
    found = []
    for c in range(index_ref.shape[0]):
        for off in (-2, -1, 0, 1, 2):
            found.append(jnp.clip(index_ref[c] + off, 0, nodes - 1))
    return found + [0, 1, nodes - 2, nodes - 1]


def padded(count):
    return -(-count // 16) * 16


def at(row):
    return slice(row, row + 1) if isinstance(row, int) else pl.ds(row, 1)


def prepare_kernel(index_ref, right_ref, inverse_ref, field_ref, coef_ref, right_t_ref, inverse_t_ref, field_t_ref, coef_t_ref, right_rows_ref, coef_rows_ref):
    right_t_ref[...] = jnp.transpose(right_ref[...])
    inverse_t_ref[...] = jnp.transpose(inverse_ref[...].astype(F32)).astype(BF16)
    field_t_ref[...] = jnp.transpose(field_ref[...])
    terms, nodes = coef_ref.shape
    found = affected(index_ref, nodes)
    right_rows_ref[...] = jnp.zeros_like(right_rows_ref)
    for j, n in enumerate(found):
        right_rows_ref[j : j + 1] = right_t_ref[at(n), :]

    @pl.when(pl.program_id(0) == 0)
    def _():
        wide = jnp.concatenate([coef_ref[...], jnp.zeros((LANES - terms, nodes), F32)], axis=0)
        coef_t_ref[...] = jnp.transpose(wide)
        coef_rows_ref[...] = jnp.zeros_like(coef_rows_ref)
        for j, n in enumerate(found):
            coef_rows_ref[j : j + 1] = coef_t_ref[at(n), :]


def prepare(index, right_side, sub_inverse, field, coefficient):
    modes, nodes = right_side.shape
    count = padded(3 * index.shape[0] + 2)
    rows = lambda width: pl.BlockSpec((LANES, width), lambda j: (j, 0))
    column = lambda height: pl.BlockSpec((height, LANES), lambda j: (0, j))
    fixed = lambda height: pl.BlockSpec((height, LANES), lambda j: (0, 0))
    return pl.pallas_call(
        prepare_kernel,
        grid=(modes // LANES,),
        in_specs=[
            SMEM,
            rows(nodes),
            rows(nodes),
            rows(nodes),
            pl.BlockSpec(coefficient.shape, lambda j: (0, 0)),
        ],
        out_specs=[column(nodes)] * 3 + [fixed(nodes), column(count), fixed(count)],
        out_shape=[
            shape((nodes, modes)),
            shape((nodes, nodes), BF16),
            shape((nodes, modes)),
            shape((nodes, LANES)),
            shape((count, modes)),
            shape((count, LANES)),
        ],
        name="prepare",
    )(index, right_side, sub_inverse, field, coefficient)


def edge_kernel(top_ref, low_ref, left_ref, right_ref, edge_ref):
    top = top_ref[...]
    before = jnp.concatenate([left_ref[:1], top[: EDGE - 1]], axis=0)
    edge_ref[:EDGE] = (2.0 * top[:EDGE] - before - top[1 : EDGE + 1]).astype(BF16)
    low = low_ref[...]
    after = jnp.concatenate([low[9:], right_ref[:1]], axis=0)
    edge_ref[EDGE:] = (2.0 * low[8:] - low[7:-1] - after).astype(BF16)


def edges(top, low, left, right):
    return pl.pallas_call(
        edge_kernel,
        in_specs=[VMEM] * 4,
        out_specs=VMEM,
        out_shape=shape((2 * EDGE, top.shape[1]), BF16),
        compiler_params=params(16384),
        name="edges",
    )(top, low, left, right)


HBM = pl.BlockSpec(memory_space=pltpu.HBM)
ANY = pl.BlockSpec(memory_space=pl.ANY)


def copies(pairs, sems):
    made = [pltpu.make_async_copy(a, b, sems.at[n]) for n, (a, b) in enumerate(pairs)]
    for copy in made:
        copy.start()
    return made


def finished(made):
    for copy in made:
        copy.wait()


def into_blocks(part_refs, blocks_ref, rows=slice(None)):
    each = part_refs[0].shape[-1] // LANES
    return [
        (part.at[:, pl.ds(b * LANES, LANES)], blocks_ref.at[n * each + b, rows])
        for n, part in enumerate(part_refs)
        for b in range(each)
    ]


def operated(blocks_ref, g_ref, pattern_ref, me, first, coefs, c):
    total = None
    own = pattern_ref.shape[2] // 4
    for k in range(g_ref.shape[0]):
        rows = []
        for t in range(g_ref.shape[2]):
            row = pattern_ref[k, t, me * own + first + c]
            owner = lax.div(row, own)
            row = (owner ^ me) * own + lax.rem(row, own)
            rows.append(blocks_ref[row])
        weights = g_ref[k, c].reshape(-1, LANES)
        product = jnp.dot(jnp.concatenate(rows, axis=1), weights, preferred_element_type=F32)
        scaled = coefs[k] * product
        total = scaled if total is None else total + scaled
    return total


def weights_into(g_ref, g_vmem, sems, first):
    return [
        pltpu.make_async_copy(g_ref.at[:, c], g_vmem.at[:, c], sems.at[first + c])
        for c in range(g_ref.shape[1])
    ]


def wait_weights(g_ref, g_vmem, sems, first, c):
    pltpu.make_async_copy(g_ref.at[:, c], g_vmem.at[:, c], sems.at[first + c]).wait()


def columns_of(coef, count):
    return [coef[:, k : k + 1] for k in range(count)]


def lanes_of(c):
    return pl.ds(pl.multiple_of(c * LANES, LANES), LANES)


def bulk_kernel(me_ref, pattern_ref, a_ref, b_ref, c_ref, d_ref, g_hbm, coef_ref, out_ref, blocks_ref, g_ref, sems):
    weights = weights_into(g_hbm, g_ref, sems, 16)
    weights[0].start()
    made = copies(into_blocks([a_ref, b_ref, c_ref, d_ref], blocks_ref), sems)
    for copy in weights[1:]:
        copy.start()
    coefs = columns_of(coef_ref[...], g_ref.shape[0])
    finished(made)

    @pl.loop(0, g_ref.shape[1])
    def _(c):
        wait_weights(g_hbm, g_ref, sems, 16, c)
        out_ref[:, lanes_of(c)] = operated(blocks_ref, g_ref, pattern_ref, me_ref[0], 0, coefs, c)


def bulk(me, pattern, parts, gblocks, coef):
    rows, modes = parts[0].shape
    return pl.pallas_call(
        bulk_kernel,
        in_specs=[SMEM, SMEM] + [ANY] * 5 + [VMEM],
        out_specs=VMEM,
        out_shape=shape((rows, modes)),
        scratch_shapes=[
            pltpu.VMEM((4 * modes // LANES, rows, LANES), BF16),
            pltpu.VMEM(gblocks.shape, BF16),
            pltpu.SemaphoreType.DMA((16 + gblocks.shape[1],)),
        ],
        compiler_params=params(52000),
        name="whole",
    )(me, pattern, *parts, gblocks, coef)


def hold_kernel(g_ref, after_ref, out_ref, sems):
    del after_ref
    made = [
        pltpu.make_async_copy(g_ref.at[:, c], out_ref.at[:, c], sems.at[c])
        for c in range(out_ref.shape[1])
    ]
    for copy in made:
        copy.start()
    finished(made)


def hold(gblocks, after, count):
    terms, _, *rest = gblocks.shape
    return pl.pallas_call(
        hold_kernel,
        in_specs=[HBM, ANY],
        out_specs=VMEM,
        out_shape=shape((terms, count, *rest), BF16),
        scratch_shapes=[pltpu.SemaphoreType.DMA((count,))],
        compiler_params=params(16384),
    )(gblocks, after)


def two_terms(value):
    high = value.astype(BF16).astype(F32)
    return high, value - high


def feed_of(rows, inverse):
    coarse = inverse.shape[0]
    inverse_t = jnp.transpose(inverse)
    feed = inverse_t[:, :1] * rows[:1]
    for c in range(1, coarse):
        feed = feed + inverse_t[:, c : c + 1] * rows[c : c + 1]
    return feed


def flags(index_ref, node):
    coarse = index_ref.shape[0]
    row = lax.broadcasted_iota(jnp.int32, (coarse, LANES), 0)
    found = jnp.zeros((coarse, LANES), F32)
    for c in range(coarse):
        found = jnp.where((row == c) & (index_ref[c] == node), 1.0, found)
    return found


def folded(row):
    count = row.shape[1] // LANES
    return jnp.concatenate([row[:, b * LANES : (b + 1) * LANES] for b in range(count)], axis=0)


def unfolded(rows):
    return jnp.concatenate([rows[b : b + 1] for b in range(rows.shape[0])], axis=1)


LAST, FIRST, NEXT = 32, 33, 48


def first_kernel(me_ref, pattern_ref, index_ref, a_ref, b_ref, c_ref, d_ref, ea_ref, eb_ref, ec_ref, ed_ref, g_hbm, coef_ref, right_ref, sub_ref, field_ref, inverse_ref, coupling_ref, message_ref, base_ref, diffs_ref, around_ref, blocks_ref, res_ref, sub_vmem, base_vmem, diffs_vmem, rows_ref, g_ref, sems):
    nodes, _ = field_ref.shape
    coarse = inverse_ref.shape[0]
    inner = pl.ds(EDGE, nodes - 2 * EDGE)
    weights = weights_into(g_hbm, g_ref, sems, 51)
    weights[0].start()
    made = copies(
        into_blocks([a_ref, b_ref, c_ref, d_ref], blocks_ref, inner)
        + into_blocks([r.at[pl.ds(0, EDGE)] for r in (ea_ref, eb_ref, ec_ref, ed_ref)], blocks_ref, pl.ds(0, EDGE))
        + into_blocks([r.at[pl.ds(EDGE, EDGE)] for r in (ea_ref, eb_ref, ec_ref, ed_ref)], blocks_ref, pl.ds(nodes - EDGE, EDGE))
        + [(right_ref, res_ref)],
        sems,
    )
    for copy in weights[1:]:
        copy.start()
    later = [
        pltpu.make_async_copy(sub_ref, sub_vmem, sems.at[49]),
        pltpu.make_async_copy(field_ref, base_vmem, sems.at[50]),
    ]
    for copy in later:
        copy.start()
    coefs = columns_of(coef_ref[...], g_ref.shape[0])
    finished(made)

    @pl.loop(0, g_ref.shape[1])
    def _(c):
        wait_weights(g_hbm, g_ref, sems, 51, c)
        total = operated(blocks_ref, g_ref, pattern_ref, me_ref[0], 0, coefs, c)
        res_ref[:, lanes_of(c)] = res_ref[:, lanes_of(c)] - total

    finished(later)
    for c in range(coarse):
        rows_ref[c : c + 1] = res_ref[pl.ds(index_ref[c], 1), :]
    feed = feed_of(rows_ref[...], inverse_ref[...])
    local = jnp.dot(sub_vmem[...], res_ref[...].astype(BF16), preferred_element_type=F32)
    base = base_vmem[...] + local
    base_vmem[...] = base
    out = [pltpu.make_async_copy(base_vmem, base_ref, sems.at[0])]
    out[0].start()
    diffs = 2.0 * base - pltpu.roll(base, 1, 0) - pltpu.roll(base, nodes - 1, 0)
    diffs_vmem[...] = diffs.astype(BF16)
    out.append(pltpu.make_async_copy(diffs_vmem, diffs_ref, sems.at[1]))
    out[1].start()

    lane = lax.broadcasted_iota(jnp.int32, (coarse, LANES), 1)
    high, low = two_terms(
        jnp.concatenate([jnp.transpose(coupling_ref[...]), jnp.zeros((coarse, LANES - coarse), F32)], axis=1)
    )
    at_last, at_first = flags(index_ref, nodes - 1), flags(index_ref, 0)
    block = high + pltpu.roll(low, coarse, 1)
    block = block + jnp.where(lane == LAST, at_last, 0.0) + jnp.where(lane == FIRST, at_first, 0.0)
    first = base[:1] + jnp.sum(at_first[:, :1] * feed.astype(BF16).astype(F32), axis=0, keepdims=True)
    edge = jnp.concatenate(
        two_terms(folded(base[nodes - 1 :])) + two_terms(folded(first)), axis=0
    )
    sent = jnp.concatenate([feed, block, edge], axis=1).astype(BF16)
    for p in range(message_ref.shape[0]):
        message_ref[p] = sent
    for j, n in enumerate(around(index_ref, nodes)):
        around_ref[j : j + 1] = base_vmem[at(n), :]
    finished(out)


def first_update(me, pattern, index, parts, edge_parts, gblocks, coef, right, sub_t, field, inverse, coupling, plane):
    nodes, modes = right.shape
    coarse = inverse.shape[0]
    return pl.pallas_call(
        first_kernel,
        in_specs=[SMEM] * 3 + [ANY] * 9 + [VMEM] + [ANY] * 3 + [VMEM] * 2,
        out_specs=[VMEM, ANY, ANY, VMEM],
        out_shape=[
            shape((plane, coarse, modes + 2 * LANES), BF16),
            shape((nodes, modes)),
            shape((nodes, modes), BF16),
            shape((padded(5 * coarse + 4), modes)),
        ],
        scratch_shapes=[
            pltpu.VMEM((4 * modes // LANES, nodes, LANES), BF16),
            pltpu.VMEM((nodes, modes), F32),
            pltpu.VMEM((nodes, nodes), BF16),
            pltpu.VMEM((nodes, modes), F32),
            pltpu.VMEM((nodes, modes), BF16),
            pltpu.VMEM((coarse, modes), F32),
            pltpu.VMEM(gblocks.shape, BF16),
            pltpu.SemaphoreType.DMA((51 + gblocks.shape[1],)),
        ],
        compiler_params=params(52000),
        name="first_update",
    )(me, pattern, index, *parts, *edge_parts, gblocks, coef, right, sub_t, field, inverse, coupling)


def advance(coupling_t, state, push):
    moved = push
    for c in range(state.shape[0]):
        moved = moved + coupling_t[:, c : c + 1] * state[c : c + 1]
    return moved


def step_of(block, coarse, at=0):
    block = block.astype(F32)
    if at:
        block = pltpu.roll(block, LANES - at, 1)
    return block + pltpu.roll(block, LANES - coarse, 1)


def lanes_and_rows(coarse):
    row = lax.broadcasted_iota(jnp.int32, (coarse, LANES), 0)
    lane = lax.broadcasted_iota(jnp.int32, (coarse, LANES), 1)
    return row, lane


def side_by_side(squares):
    coarse = squares[0].shape[0]
    _, lane = lanes_and_rows(coarse)
    total = None
    for n, square in enumerate(squares):
        square = jnp.where(lane < coarse, square, 0.0)
        square = pltpu.roll(square, n * coarse, 1) if n else square
        total = square if total is None else total + square
    return total


def terms_of(weights):
    return jnp.concatenate(two_terms(weights), axis=0).astype(BF16)


def plane_kernel(feeds_ref, out_ref, weights_ref):
    plane, coarse, width = feeds_ref.shape
    modes = width - 2 * LANES
    row, lane = lanes_and_rows(coarse)
    one = (row == lane).astype(F32)
    whole, wholes = one, []
    for q in range(plane - 1, -1, -1):
        wholes.append(whole)
        whole = advance(whole, step_of(feeds_ref[q, :, modes : modes + LANES], coarse), jnp.zeros_like(one))
    totals = terms_of(side_by_side(wholes[::-1]))
    weights_ref[...] = totals
    feeds = feeds_ref[:, :, :modes].reshape(plane * coarse, modes)
    sums = jnp.dot(totals, feeds, preferred_element_type=F32)
    state = sums[:coarse] + sums[coarse:]
    matrix = jnp.where(lane < coarse, whole, 0.0)
    high, low = two_terms(matrix)
    first = feeds_ref[0, :, modes : modes + LANES].astype(F32)
    final = feeds_ref[plane - 1, :, modes : modes + LANES].astype(F32)
    block = high + pltpu.roll(low, coarse, 1)
    block = block + jnp.where(lane == LAST, final, 0.0) + jnp.where(lane == FIRST, first, 0.0)
    block = block + jnp.where((lane >= NEXT) & (lane < NEXT + 2 * coarse), pltpu.roll(first, NEXT, 1), 0.0)
    edge = jnp.where(
        row < coarse // 2,
        feeds_ref[plane - 1, :, modes + LANES :].astype(F32),
        feeds_ref[0, :, modes + LANES :].astype(F32),
    )
    sent = jnp.concatenate([state, block, edge], axis=1).astype(BF16)
    for z in range(out_ref.shape[0]):
        out_ref[z] = sent


def plane_totals(feeds, planes):
    plane, coarse, width = feeds.shape
    return pl.pallas_call(
        plane_kernel,
        in_specs=[VMEM],
        out_specs=[VMEM] * 2,
        out_shape=[
            shape((planes, coarse, width), BF16),
            shape((2 * coarse, plane * coarse), BF16),
        ],
        compiler_params=params(52000),
        name="plane_totals",
    )(feeds)


def inside_kernel(p_ref, feeds_ref, totals_ref, inside_ref, weights_ref, carry_ref):
    plane, coarse, width = feeds_ref.shape
    modes = width - 2 * LANES
    p = p_ref[0]
    row, lane = lanes_and_rows(coarse)
    one = (row == lane).astype(F32)
    before, befores = jnp.zeros_like(one), []
    for q in range(plane - 1, -1, -1):
        before = jnp.where(q == p - 1, one, before)
        befores.append(before)
        before = advance(before, step_of(feeds_ref[q, :, modes : modes + LANES], coarse), jnp.zeros_like(one))
    carry_ref[...] = jnp.where(p == 0, one, before)
    excluding = side_by_side(befores[::-1])
    own = step_of(feeds_ref[p, :, modes : modes + LANES], coarse)
    including = advance(own, excluding, (lane == p * coarse + row).astype(F32))
    weights_ref[...] = jnp.concatenate([totals_ref[...], terms_of(including)], axis=0)
    feeds = feeds_ref[:, :, :modes].reshape(plane * coarse, modes)
    sums = jnp.dot(terms_of(excluding), feeds, preferred_element_type=F32)
    inside_ref[...] = sums[:coarse] + sums[coarse:]


def inside_plane(p, feeds, totals):
    plane, coarse, width = feeds.shape
    return pl.pallas_call(
        inside_kernel,
        in_specs=[SMEM, VMEM, VMEM],
        out_specs=[VMEM] * 3,
        out_shape=[
            shape((coarse, width - 2 * LANES)),
            shape((4 * coarse, plane * coarse), BF16),
            shape((coarse, LANES)),
        ],
        compiler_params=params(52000),
        name="inside_plane",
    )(p, feeds, totals)


def second_plane_kernel(feeds_ref, weights_ref, out_ref, inside_ref):
    plane, coarse, modes = feeds_ref.shape
    feeds = feeds_ref[...].reshape(plane * coarse, modes)
    sums = jnp.dot(weights_ref[...], feeds, preferred_element_type=F32)
    state = (sums[:coarse] + sums[coarse : 2 * coarse]).astype(BF16)
    inside_ref[...] = sums[2 * coarse : 3 * coarse] + sums[3 * coarse :]
    for z in range(out_ref.shape[0]):
        out_ref[z] = state


def second_plane_totals(feeds, weights, planes):
    _, coarse, modes = feeds.shape
    return pl.pallas_call(
        second_plane_kernel,
        in_specs=[VMEM] * 2,
        out_specs=[VMEM] * 2,
        out_shape=[shape((planes, coarse, modes), BF16), shape((coarse, modes))],
        compiler_params=params(52000),
        name="second_plane_totals",
    )(feeds, weights)


def correct_kernel(z_ref, p_ref, index_ref, feeds_ref, totals_ref, inside_ref, carry_ref, around_ref, sent_ref, error_ref, weights_ref, wide_ref, rows_ref):
    nodes, modes = wide_ref.shape[0] - 16, wide_ref.shape[1]
    plane, planes = feeds_ref.shape[0], totals_ref.shape[0]
    z, p = z_ref[0], p_ref[0]
    coarse = index_ref.shape[0]
    none = jnp.zeros((coarse, LANES), F32)
    factor = none
    factors = []
    for q in range(planes - 1, -1, -1):
        factor = jnp.where(q == z - 1, carry_ref[...], factor)
        factors.append(factor)
        factor = advance(factor, step_of(totals_ref[q, :, modes : modes + LANES], coarse), none)
    weights = side_by_side(factors[::-1])
    totals = totals_ref[:, :, :modes].reshape(planes * coarse, modes)
    sums = jnp.dot(terms_of(weights), totals, preferred_element_type=F32)
    before = inside_ref[...] + sums[:coarse] + sums[coarse:]
    own = step_of(feeds_ref[p, :, modes : modes + LANES], coarse)
    error = advance(own, before, feeds_ref[p, :, :modes].astype(F32))
    weights_ref[...] = terms_of(advance(own, weights, none))

    block, edge = slice(modes, modes + LANES), slice(modes + LANES, modes + 2 * LANES)
    p_left, z_left = jnp.maximum(p - 1, 0), jnp.maximum(z - 1, 0)
    p_right, z_right = jnp.minimum(p + 1, plane - 1), jnp.minimum(z + 1, planes - 1)
    here = p > 0
    left_block = jnp.where(here, feeds_ref[p_left, :, block].astype(F32), totals_ref[z_left, :, block].astype(F32))
    left_edge = jnp.where(here, feeds_ref[p_left, :, edge].astype(F32), totals_ref[z_left, :, edge].astype(F32))
    left = unfolded(left_edge[:4] + left_edge[4:8])
    left = left + jnp.sum(left_block[:, LAST : LAST + 1] * before, axis=0, keepdims=True)
    left = jnp.where((z > 0) | here, left, 0.0)
    here = p < plane - 1
    near, far = feeds_ref[p_right, :, block], totals_ref[z_right, :, block]
    step = jnp.where(here, step_of(near, coarse), step_of(far, coarse, NEXT))
    flag = jnp.where(here, near.astype(F32), far.astype(F32))
    right_edge = jnp.where(here, feeds_ref[p_right, :, edge].astype(F32), totals_ref[z_right, :, edge].astype(F32))
    moved = advance(step, error, jnp.zeros_like(error))
    right = unfolded(right_edge[8:12] + right_edge[12:])
    right = right + jnp.sum(flag[:, FIRST : FIRST + 1] * moved, axis=0, keepdims=True)
    right = jnp.where((z < planes - 1) | here, right, 0.0)

    error_ref[...] = error
    for j, n in enumerate(around(index_ref, nodes)):
        wide_ref[at(8 + n), :] = around_ref[j : j + 1]
    wide_ref[7:8] = left
    wide_ref[8 + nodes : 9 + nodes] = right
    for c in range(coarse):
        row = pl.ds(8 + index_ref[c], 1)
        wide_ref[row, :] = wide_ref[row, :] + error[c : c + 1]
    found = affected(index_ref, nodes)
    rows_ref[...] = jnp.zeros_like(rows_ref)
    for j, n in enumerate(found):
        rows_ref[j : j + 1] = (
            2.0 * wide_ref[at(8 + n), :] - wide_ref[at(7 + n), :] - wide_ref[at(9 + n), :]
        )
    sent_ref[...] = rows_ref[...].astype(BF16)


def correct(z, p, index, feeds, totals, inside, carry, near, nodes):
    modes = near.shape[1]
    coarse = index.shape[0]
    rows = padded(3 * coarse + 2)
    return pl.pallas_call(
        correct_kernel,
        in_specs=[SMEM] * 3 + [VMEM] * 5,
        out_specs=[VMEM] * 3,
        out_shape=[
            shape((rows, modes), BF16),
            shape((coarse, modes)),
            shape((2 * coarse, totals.shape[0] * coarse), BF16),
        ],
        scratch_shapes=[pltpu.VMEM((nodes + 16, modes), F32), pltpu.VMEM((rows, modes), F32)],
        compiler_params=params(52000),
        name="correct",
    )(z, p, index, feeds, totals, inside, carry, near)


def redo_kernel(me_ref, pattern_ref, a_ref, b_ref, c_ref, d_ref, g_ref, coef_ref, right_ref, inverse_ref, message_ref, res_ref, blocks_ref, rows_ref, sems):
    made = copies(into_blocks([a_ref, b_ref, c_ref, d_ref], blocks_ref), sems)
    coefs = columns_of(coef_ref[...], g_ref.shape[0])
    finished(made)

    @pl.loop(0, g_ref.shape[1])
    def _(c):
        total = operated(blocks_ref, g_ref, pattern_ref, me_ref[0], 0, coefs, c)
        res_ref[:, lanes_of(c)] = right_ref[:, lanes_of(c)] - total

    for c in range(inverse_ref.shape[0]):
        rows_ref[c : c + 1] = res_ref[3 * c + 1 : 3 * c + 2]
    feed = feed_of(rows_ref[...], inverse_ref[...]).astype(BF16)
    for p in range(message_ref.shape[0]):
        message_ref[p] = feed


def redo(me, pattern, parts, gblocks, coef_rows, right_rows, inverse, plane):
    rows, modes = right_rows.shape
    coarse = inverse.shape[0]
    return pl.pallas_call(
        redo_kernel,
        in_specs=[SMEM] * 2 + [ANY] * 4 + [VMEM] * 4,
        out_specs=[VMEM] * 2,
        out_shape=[shape((plane, coarse, modes), BF16), shape((rows, modes))],
        scratch_shapes=[
            pltpu.VMEM((4 * modes // LANES, rows, LANES), BF16),
            pltpu.VMEM((coarse, modes), F32),
            pltpu.SemaphoreType.DMA((16,)),
        ],
        compiler_params=params(52000),
        name="redo",
    )(me, pattern, *parts, gblocks, coef_rows, right_rows, inverse)


def last_local_kernel(index_ref, op_ref, right_ref, rows_ref, sub_ref, base_ref, error_ref, base_out_ref, res_out_ref, res_ref, field_ref):
    nodes = op_ref.shape[0]
    res_ref[...] = right_ref[...] - op_ref[...]
    for j, n in enumerate(affected(index_ref, nodes)):
        res_ref[at(n), :] = rows_ref[j : j + 1]
    res = res_ref[...]
    field_ref[...] = base_ref[...] + jnp.dot(sub_ref[...], res.astype(BF16), preferred_element_type=F32)
    for c in range(error_ref.shape[0]):
        field_ref[at(index_ref[c]), :] = field_ref[at(index_ref[c]), :] + error_ref[c : c + 1]
    base_out_ref[...] = jnp.transpose(field_ref[...])
    res_out_ref[...] = jnp.transpose(res)


def last_local(index, op, right, rows, sub_t, base, error):
    nodes, modes = op.shape
    column = lambda height: pl.BlockSpec((height, LANES), lambda j: (0, j))
    row = pl.BlockSpec((LANES, nodes), lambda j: (j, 0))
    return pl.pallas_call(
        last_local_kernel,
        grid=(modes // LANES,),
        in_specs=[
            SMEM,
            column(nodes),
            column(nodes),
            column(rows.shape[0]),
            pl.BlockSpec((nodes, nodes), lambda j: (0, 0)),
            column(nodes),
            column(error.shape[0]),
        ],
        out_specs=[row, row],
        out_shape=[shape((modes, nodes)), shape((modes, nodes))],
        scratch_shapes=[pltpu.VMEM((nodes, LANES), F32), pltpu.VMEM((nodes, LANES), F32)],
        name="last_local",
    )(index, op, right, rows, sub_t, base, error)


def last_kernel(index_ref, totals_ref, inside_ref, weights_ref, base_ref, out_ref, base_vmem, out_vmem, sems):
    modes, nodes = base_ref.shape
    rows_of = lambda n: pl.ds(n * LANES, LANES)
    loads = [
        pltpu.make_async_copy(base_ref.at[rows_of(n)], base_vmem.at[rows_of(n)], sems.at[n])
        for n in range(modes // LANES)
    ]
    for load in loads:
        load.start()
    planes, coarse, _ = totals_ref.shape
    totals = totals_ref[...].reshape(planes * coarse, modes)
    sums = jnp.dot(weights_ref[...], totals, preferred_element_type=F32)
    error = inside_ref[...] + sums[:coarse] + sums[coarse:]
    high = error.astype(BF16).astype(F32)
    rest = error - high
    mid = rest.astype(BF16).astype(F32)
    terms = jnp.transpose(jnp.concatenate([high, mid, rest - mid], axis=0)).astype(BF16)
    node = lax.broadcasted_iota(jnp.int32, (coarse, nodes), 1)
    row = lax.broadcasted_iota(jnp.int32, (coarse, nodes), 0)
    wanted = jnp.zeros((coarse, nodes), jnp.int32)
    for c in range(coarse):
        wanted = jnp.where(row == c, index_ref[c], wanted)
    onehot = (node == wanted).astype(F32)
    onehot = jnp.concatenate([onehot] * 3, axis=0).astype(BF16)
    made = []
    for n in range(modes // LANES):
        rows = slice(n * LANES, (n + 1) * LANES)
        loads[n].wait()
        out_vmem[rows] = base_vmem[rows] + jnp.dot(terms[rows], onehot, preferred_element_type=F32)
        made.append(pltpu.make_async_copy(out_vmem.at[rows], out_ref.at[rows], sems.at[modes // LANES + n]))
        made[-1].start()
    finished(made)


def last(index, totals, inside, weights, base):
    modes, _ = base.shape
    return pl.pallas_call(
        last_kernel,
        in_specs=[SMEM] + [VMEM] * 3 + [ANY],
        out_specs=ANY,
        out_shape=shape(base.shape),
        scratch_shapes=[
            pltpu.VMEM(base.shape, F32),
            pltpu.VMEM(base.shape, F32),
            pltpu.SemaphoreType.DMA((2 * modes // LANES,)),
        ],
        input_output_aliases={4: 0},
        compiler_params=params(52000),
        name="last",
    )(index, totals, inside, weights, base)


def from_neighbours(last_rows, first_rows):
    size = lax.axis_size(SUB)
    up = [(i, i + 1) for i in range(size - 1)]
    left = lax.ppermute(last_rows, SUB, up)
    right = lax.ppermute(first_rows, SUB, [(j, i) for i, j in up])
    return left, right


def over_modes(own):
    swap = [(0, 1), (1, 0)]
    across = lax.ppermute(own, "yl", swap)
    beside = lax.ppermute(own, "core", swap)
    onward = lax.ppermute(across, "core", swap)
    return own, beside, across, onward


def over_modes_directly(own):
    across = lax.ppermute(own, "yl", [(0, 1), (1, 0)])
    diagonal = lax.ppermute(own, MODE, [(0, 3), (1, 2), (2, 1), (3, 0)])
    beside = lax.ppermute(own, "core", [(0, 1), (1, 0)])
    return own, beside, across, diagonal


def shards(right_side, start_field, coefficient, gblocks, pattern, sub_inverse, coarse_index, coarse_inv, coupling):
    me = lax.axis_index(MODE).reshape(1)
    z, p = lax.axis_index("z").reshape(1), lax.axis_index(PLANE).reshape(1)
    planes, plane = lax.axis_size("z"), lax.axis_size(PLANE)
    nodes = start_field.shape[1]
    pattern = jnp.swapaxes(pattern, 1, 2)
    diffs, top, low, last_rows, first_rows = start(start_field)
    parts = over_modes(diffs)
    left, right = from_neighbours(last_rows, first_rows)
    edge_rows = edges(top, low, left, right)
    edge_parts = over_modes_directly(edge_rows)
    rhs, sub_t, field, coef, right_rows, coef_rows = prepare(
        coarse_index, right_side, sub_inverse, start_field, coefficient
    )
    message, base, diffs, near = first_update(
        me, pattern, coarse_index, parts, edge_parts, gblocks, coef, rhs, sub_t, field, coarse_inv, coupling, plane
    )
    parts = over_modes(diffs)
    feeds = lax.all_to_all(message, PLANE, 0, 0, tiled=True)
    totals, weights = plane_totals(feeds, planes)
    inside, weights, carry = inside_plane(p, feeds, weights)
    totals = lax.all_to_all(totals, "z", 0, 0, tiled=True)
    rows, error, plane_weights = correct(z, p, coarse_index, feeds, totals, inside, carry, near, nodes)
    rows = over_modes_directly(rows)
    op = bulk(me, pattern, parts, gblocks, coef)
    held = hold(gblocks, error, gblocks.shape[1])
    message, res_rows = redo(me, pattern, rows, held, coef_rows, right_rows, coarse_inv, plane)
    later = lax.all_to_all(message, PLANE, 0, 0, tiled=True)
    base, residual = last_local(coarse_index, op, rhs, res_rows, sub_t, base, error)
    later_totals, inside = second_plane_totals(later, weights, planes)
    later_totals = lax.all_to_all(later_totals, "z", 0, 0, tiled=True)
    field = last(coarse_index, later_totals, inside, plane_weights, base)
    return field, residual


def solution(mesh):
    split = Mesh(mesh.devices.reshape(8, 4, 2, 2, 2), SUB + MODE)
    placed = (
        P(MODE, SUB),
        P(MODE, SUB),
        P(None, SUB),
        P(None, MODE, None, None, None),
        P(),
        P(SUB, None),
        P(SUB),
        P(SUB, None),
        P(SUB, None),
    )
    return jax.shard_map(shards, mesh=split, in_specs=placed, out_specs=(P(MODE, SUB), P(MODE, SUB)), check_vma=False)
```
